32 devices in a mesh: groups: 2 (over y), stripe: 8 (over z, x), exp: 2 (over core).
Axes of the slice: x: 2, y: 2, z: 4, core: 2. Of those that a mesh axis runs over, the one named last changes fastest.
Arguments:
- template: float32 [256, 2048], P(('groups', 'stripe'), 'exp'), parts along dimension 0, may hold values from -6 to 6
- exposure: float32 [4, 128, 2048], P(('groups', 'exp'), 'stripe'), parts along dimension 0, may hold values from -30 to 30
- cosmic_mask: int32 [4, 128, 2048], P(('groups', 'exp'), 'stripe'), parts along dimension 0, may hold values 0 or 1
- stamp_blocks: int32 [16, 16], P(('groups', 'stripe')), parts along dimension 0, may hold values from 0 to 31, as said below
- row_filters: float32 [19, 19], replicated, may hold values from -1 to 2.5
- col_filters: float32 [19, 19], replicated, may hold values from -1 to 2.5
Outputs:
- filtered: float32 [4, 128, 2048], P(('groups', 'exp'), 'stripe'), parts along dimension 0
- coefficients: float32 [4, 64], P(('groups', 'exp')), parts along dimension 0
The draws below stay inside these ranges and needn't reach their ends.
There are 2 independent parts, one for each index of `groups`. The reference program is written for one: setup_inputs(seed, part) draws one part's arguments, and reference() takes and returns one part's arrays. A program takes and returns all parts, laid end to end along the dimension named above; an argument that names none is the same for every part. Nothing has to cross between parts.
Inputs may be any that keep to these rules, and one draw needn't show every extreme that they name: `stamp_blocks`: each row lists the stamps of one stripe; stamp j lies in column block 2 j or 2 j + 1.
All inputs are finite; a program needn't handle non-finite values. No bound on the sum of `cosmic_mask` on one device may be relied on, other than what follows from the above.
Results may differ from the reference program's by a relative error of at most 0.0003.
Values sent between devices are 32-bit elements; how exact they have to be, the bound alone decides.
A program may use at most 64 MiB of HBM per device.

```python
import math
import jax
import jax.numpy as jnp
from jax import lax

ROWS_DEV = 16
COLS = 2048
HALF = 9
BASES = 19
STAMP_W = 64
TAPS = 19
NCOL = 64
NSTAMP = 16
STRIPES = 8
NR = 128
NEXP = 2


def sky_field(key):
    return jnp.clip(jax.random.normal(jax.random.fold_in(key, 101), (NR, COLS), jnp.float32), -5.0, 5.0)


def draw_template(key, part):
    sky = sky_field(key)
    extra = jnp.clip(jax.random.normal(jax.random.fold_in(key, 103), (NR, COLS), jnp.float32), -5.0, 5.0)
    return sky + 0.1 * extra


def blur_axis(field, near, far, axis_id):
    centre = 1.0 - 2.0 * near - 2.0 * far
    result = centre * field + near * (jnp.roll(field, 1, axis_id) + jnp.roll(field, -1, axis_id))
    return result + far * (jnp.roll(field, 2, axis_id) + jnp.roll(field, -2, axis_id))


def draw_exposure(key, part):
    sky = sky_field(key)
    row_pos = (2.0 * jnp.arange(NR, dtype=jnp.float32) + 1.0) / NR - 1.0
    col_pos = (2.0 * jnp.arange(COLS, dtype=jnp.float32) + 1.0) / COLS - 1.0
    amplitude = (1.3 + row_pos + 0.8 * row_pos * row_pos)[:, None] * (1.0 + 0.4 * jnp.cos(3.0 * math.pi * col_pos))[None, :]
    frames = []
    for frame in range(NEXP):
        frame_key = jax.random.fold_in(key, 200 + frame)
        params = jax.random.uniform(frame_key, (5,), jnp.float32)
        blurred = blur_axis(sky, 0.15 + 0.15 * params[0], 0.02 + 0.08 * params[1], 0)
        blurred = blur_axis(blurred, 0.15 + 0.15 * params[2], 0.02 + 0.08 * params[3], 1)
        jitter = 0.3 * jnp.clip(jax.random.normal(jax.random.fold_in(frame_key, 7), (NR, COLS), jnp.float32), -5.0, 5.0)
        offset_level = 0.5 * params[4] + 0.4 * col_pos[None, :] + 0.3 * row_pos[:, None] * col_pos[None, :]
        frames.append(amplitude * blurred + offset_level + jitter)
    return jnp.stack(frames)


def filter_bank(key, salt):
    taps_pos = jnp.arange(TAPS, dtype=jnp.float32) - HALF
    sigma = jnp.exp(jax.random.uniform(jax.random.fold_in(key, salt), (BASES, 1), jnp.float32, math.log(0.6), math.log(3.5)))
    profile = jnp.exp(-taps_pos[None, :] ** 2 / (2.0 * sigma * sigma)) / (2.5 * sigma)
    first = jnp.clip(jax.random.normal(jax.random.fold_in(key, salt + 1), (BASES, TAPS), jnp.float32), -4.0, 4.0)
    second = jnp.clip(jax.random.normal(jax.random.fold_in(key, salt + 2), (BASES, TAPS), jnp.float32), -4.0, 4.0)
    return profile * (1.0 + 0.3 * first) + 0.12 * second


def draw_row_filters(key, part):
    return filter_bank(key, 301)


def draw_col_filters(key, part):
    return filter_bank(key, 311)


def draw_stamp_blocks(key, part):
    choose = jax.random.randint(jax.random.fold_in(key, 401), (STRIPES, NSTAMP), 0, 2)
    row_id = jnp.arange(STRIPES, dtype=jnp.int32)[:, None]
    slot_id = jnp.arange(NSTAMP, dtype=jnp.int32)[None, :]
    choose = jnp.where((row_id == 0) & (slot_id == 0), 0, choose)
    choose = jnp.where((row_id == 0) & (slot_id == NSTAMP - 1), 1, choose)
    return (2 * slot_id + choose).astype(jnp.int32)


def touch_ends(drawn, own_key, least, largest):
    longest = drawn.shape.index(max(drawn.shape))
    spots = []
    for shift in (0, 1):
        where = [jax.random.randint(jax.random.fold_in(own_key, axis), (), 0, length) for axis, length in enumerate(drawn.shape)]
        where[longest] = (where[longest] + shift) % drawn.shape[longest]
        spots.append(tuple(where))
    return drawn.at[spots[0]].set(least).at[spots[1]].set(largest)


def setup_inputs(seed: int = 0, part: int = 0) -> dict:
    key_of = jax.random.split(jax.random.key(seed), 7)
    own_keys = jax.random.split(jax.random.fold_in(key_of[6], part), 7)
    return {
        "template": draw_template(jax.random.fold_in(jax.random.fold_in(key_of[6], part), 71), part),
        "exposure": draw_exposure(jax.random.fold_in(jax.random.fold_in(key_of[6], part), 71), part),
        "cosmic_mask": touch_ends((jax.random.randint(own_keys[2], (NEXP, NR, COLS), 0, 32) < 31).astype(jnp.int32), jax.random.fold_in(own_keys[2], 1), 0, 1),
        "stamp_blocks": draw_stamp_blocks(jax.random.fold_in(jax.random.fold_in(key_of[6], part), 71), part),
        "row_filters": draw_row_filters(jax.random.fold_in(key_of[6], 71), part),
        "col_filters": draw_col_filters(jax.random.fold_in(key_of[6], 71), part),
    }


def stripe_bases(extended, row_filters, col_filters):
    row_span = extended.shape[0] - 2 * HALF
    col_span = extended.shape[1] - 2 * HALF
    vertical = row_filters[:, 0, None, None] * extended[None, 0:row_span, :]
    for offset in range(1, 2 * HALF + 1):
        vertical = vertical + row_filters[:, offset, None, None] * extended[None, offset:offset + row_span, :]
    result = col_filters[:, 0, None, None] * vertical[:, :, 0:col_span]
    for offset in range(1, 2 * HALF + 1):
        result = result + col_filters[:, offset, None, None] * vertical[:, :, offset:offset + col_span]
    return result

def background_terms(horiz_pos, vert_pos):
    constant = jnp.ones_like(horiz_pos)
    u_square = 0.5 * (3.0 * horiz_pos * horiz_pos - 1.0)
    v_square = 0.5 * (3.0 * vert_pos * vert_pos - 1.0)
    return jnp.stack([constant, horiz_pos, vert_pos, horiz_pos * vert_pos, u_square, v_square, horiz_pos * v_square])

def design_matrix(picked, horiz_pos, vert_pos):
    kernel = jnp.stack([picked, picked * horiz_pos, picked * vert_pos], axis=1).reshape(3 * picked.shape[0], -1)
    background = background_terms(horiz_pos, vert_pos).reshape(7, -1)
    return jnp.concatenate([kernel, background], axis=0).astype(jnp.bfloat16)

def solve_normal(normal_aug):
    factor = jnp.linalg.cholesky(normal_aug[:, :-1])
    lower_sol = jax.scipy.linalg.solve_triangular(factor, normal_aug[:, -1], lower=True)
    return jax.scipy.linalg.solve_triangular(factor, lower_sol, lower=True, trans=1)

def model_values(bases, solution, horiz_pos, vert_pos):
    kernel_part = solution[:3 * BASES].reshape(BASES, 3)
    steady = jnp.einsum('bij,b->ij', bases, kernel_part[:, 0], precision=lax.Precision.HIGHEST)
    along_u = jnp.einsum('bij,b->ij', bases, kernel_part[:, 1], precision=lax.Precision.HIGHEST)
    along_v = jnp.einsum('bij,b->ij', bases, kernel_part[:, 2], precision=lax.Precision.HIGHEST)
    background = background_terms(horiz_pos, vert_pos)
    level = jnp.einsum('mij,m->ij', background, solution[3 * BASES:], precision=lax.Precision.HIGHEST)
    return steady + horiz_pos * along_u + vert_pos * along_v + level

def reference(template, exposure, cosmic_mask, stamp_blocks, row_filters, col_filters):
    padded = jnp.pad(template, ((HALF, HALF), (HALF, HALF)))
    col_index = jnp.arange(COLS, dtype=jnp.int32)
    horiz_all = (2.0 * col_index.astype(jnp.float32) + 1.0) / COLS - 1.0
    offsets = jnp.arange(STAMP_W, dtype=jnp.int32)

    def stripe_rows(stripe_id):
        row_index = stripe_id * ROWS_DEV + jnp.arange(ROWS_DEV, dtype=jnp.int32)
        return (2.0 * row_index.astype(jnp.float32) + 1.0) / NR - 1.0

    def fit_stripe(normal_sum, stripe_id):
        extended = lax.dynamic_slice_in_dim(padded, (stripe_id * ROWS_DEV).astype(jnp.int32), ROWS_DEV + 2 * HALF, 0)
        bases = stripe_bases(extended, row_filters, col_filters)
        blocks = lax.dynamic_index_in_dim(stamp_blocks, stripe_id, 0, keepdims=False)
        chosen = (blocks[:, None] * STAMP_W + offsets[None, :]).reshape(-1).astype(jnp.int32)
        picked = jnp.take(bases, chosen, axis=2)
        horiz_pos = jnp.broadcast_to(horiz_all[chosen][None, :], (ROWS_DEV, chosen.shape[0]))
        vert_pos = jnp.broadcast_to(stripe_rows(stripe_id)[:, None], (ROWS_DEV, chosen.shape[0]))
        design = design_matrix(picked, horiz_pos, vert_pos)
        science = lax.dynamic_slice_in_dim(exposure, (stripe_id * ROWS_DEV).astype(jnp.int32), ROWS_DEV, 1)
        good = lax.dynamic_slice_in_dim(cosmic_mask, (stripe_id * ROWS_DEV).astype(jnp.int32), ROWS_DEV, 1)
        science_sel = jnp.take(science, chosen, axis=2)
        good_sel = jnp.take(good, chosen, axis=2).astype(jnp.float32)
        weighted = design[None] * good_sel.reshape(NEXP, 1, -1).astype(jnp.bfloat16)
        target = (good_sel * science_sel).reshape(NEXP, 1, -1).astype(jnp.bfloat16)
        augmented = jnp.concatenate([weighted, target], axis=1)
        normal = jnp.einsum('enp,emp->enm', weighted.astype(jnp.float32), augmented.astype(jnp.float32), precision=lax.Precision.HIGHEST)
        return (normal_sum + normal, None)
    start_sum = jnp.zeros((NEXP, NCOL, NCOL + 1), jnp.float32)
    normal_total, _ = lax.scan(fit_stripe, start_sum, jnp.arange(STRIPES, dtype=jnp.int32))
    coefficients = jax.vmap(solve_normal)(normal_total)

    def model_stripe(stripe_id):
        extended = lax.dynamic_slice_in_dim(padded, (stripe_id * ROWS_DEV).astype(jnp.int32), ROWS_DEV + 2 * HALF, 0)
        bases = stripe_bases(extended, row_filters, col_filters)
        horiz_pos = jnp.broadcast_to(horiz_all[None, :], (ROWS_DEV, COLS))
        vert_pos = jnp.broadcast_to(stripe_rows(stripe_id)[:, None], (ROWS_DEV, COLS))
        models = jax.vmap(lambda solution: model_values(bases, solution, horiz_pos, vert_pos))(coefficients)
        science = lax.dynamic_slice_in_dim(exposure, (stripe_id * ROWS_DEV).astype(jnp.int32), ROWS_DEV, 1)
        good = lax.dynamic_slice_in_dim(cosmic_mask, (stripe_id * ROWS_DEV).astype(jnp.int32), ROWS_DEV, 1)
        return good.astype(jnp.float32) * (science - models)
    stacked = lax.map(model_stripe, jnp.arange(STRIPES, dtype=jnp.int32))
    difference = jnp.transpose(stacked, (1, 0, 2, 3)).reshape(NEXP, NR, COLS)
    framed = jnp.pad(difference, ((0, 0), (1, 1), (1, 1)))
    neighbours = framed[:, 2:, 1:-1] + framed[:, :-2, 1:-1] + framed[:, 1:-1, 2:] + framed[:, 1:-1, :-2]
    filtered = 4.0 * difference - neighbours
    return (filtered, coefficients)
```

```python
import functools

import jax
import jax.numpy as jnp
from jax import lax
from jax.experimental import pallas as pl
from jax.experimental.pallas import tpu as pltpu
from jax.sharding import PartitionSpec as P

HALF = 9
STAMP_W = 64
EDGE = 128
HIGHEST = lax.Precision.HIGHEST
MESH = pl.DeviceIdType.MESH


def round_up(n, m):
    return -(-n // m) * m


def row_coords(first, count, region_rows):
    index = lax.broadcasted_iota(jnp.int32, (count, 1), 0).astype(jnp.float32) + first
    return (2.0 * index + 1.0) / region_rows - 1.0


def col_coords(first, count, col_total):
    index = lax.broadcasted_iota(jnp.int32, (1, count), 1).astype(jnp.float32) + first
    return (2.0 * index + 1.0) / col_total - 1.0


def background(u, v):
    uu = 0.5 * (3.0 * u * u - 1.0)
    vv = 0.5 * (3.0 * v * v - 1.0)
    return [None, u, v, u * v, uu, vv, u * vv]


def normal_kernel(region_rows, band_ref, ext_ref, exp_ref, mask_ref, par_ref, col_ref, out_ref, vert, design):
    bases = col_ref.shape[0]
    taps = col_ref.shape[1]
    rows, cols = exp_ref.shape
    wide = ext_ref.shape[1]
    fit = 3 * bases + 7
    half_cols = cols // 2
    blocks = half_cols // EDGE
    vert[...] = jnp.dot(band_ref[...], ext_ref[...], precision=HIGHEST, preferred_element_type=jnp.float32)
    low = lax.broadcasted_iota(jnp.int32, (1, EDGE), 1) < STAMP_W

    def pick(x):
        parts = []
        for m in range(cols // (2 * EDGE)):
            a = x[:, 2 * m * EDGE : (2 * m + 1) * EDGE]
            b = x[:, (2 * m + 1) * EDGE : (2 * m + 2) * EDGE]
            upper = par_ref[:, m * EDGE : (m + 1) * EDGE] > 0.5
            mine = jnp.where(low, a, b)
            other = pltpu.roll(jnp.where(low, b, a), STAMP_W, 1)
            parts.append(jnp.where(upper == low, other, mine))
        return jnp.concatenate(parts, axis=1)

    first = (lax.axis_index("stripe") * rows).astype(jnp.float32)
    v = jnp.broadcast_to(row_coords(first, rows, region_rows), (rows, half_cols))
    u_all = jnp.broadcast_to(col_coords(0.0, cols, cols), (8, cols))
    u = jnp.broadcast_to(pick(u_all)[0:1], (rows, half_cols))
    good = pick(mask_ref[...].astype(jnp.float32))

    def put(n, x):
        x = x * good
        for m in range(blocks):
            design[m, pl.ds(pl.multiple_of(n * rows, rows), rows), :] = x[:, m * EDGE : (m + 1) * EDGE]

    def each_basis(b, carry):
        x = vert[pl.ds(pl.multiple_of(b * rows, rows), rows), :]
        acc = jnp.zeros((rows, cols), jnp.float32)
        for j in range(taps):
            acc = acc + col_ref[b, j] * pltpu.roll(x, wide - (EDGE - HALF) - j, 1)[:, :cols]
        picked = pick(acc)
        put(3 * b, picked)
        put(3 * b + 1, picked * u)
        put(3 * b + 2, picked * v)
        return carry

    lax.fori_loop(0, bases, each_basis, 0)
    terms = background(u, v)
    terms[0] = jnp.ones_like(u)
    for m, term in enumerate(terms):
        put(3 * bases + m, term)
    put(fit, pick(exp_ref[...]))
    total = out_ref.shape[0]
    for n in range(fit + 1, total):
        put(n, jnp.zeros_like(u))
    acc = jnp.zeros((total, total), jnp.float32)
    for r in range(rows):
        x = [design[m, pl.ds(r, total, stride=rows), :] for m in range(blocks)]
        x = jnp.concatenate(x, axis=1).astype(jnp.bfloat16)
        acc = acc + lax.dot_general(x, x, (((1,), (1,)), ((), ())), preferred_element_type=jnp.float32)
    out_ref[...] = jnp.concatenate([acc, jnp.zeros((total, EDGE - total), jnp.float32)], axis=1)


def solve_kernel(count, fit, local_ref, out_ref, row_ref, send, held, send_sem, recv_sem):
    me = lax.axis_index("stripe")
    steps = []
    d = 1
    while d < count:
        steps.append(d)
        d *= 2
    partners = [me + d * (1 - 2 * ((me // d) % 2)) for d in steps]
    barrier = pltpu.get_barrier_semaphore()
    for partner in partners:
        pl.semaphore_signal(barrier, inc=1, device_id={"stripe": partner}, device_id_type=MESH)
    pl.semaphore_wait(barrier, len(partners))
    total = local_ref[...]
    for s, partner in enumerate(partners):
        source = local_ref
        if s:
            send[s] = total
            source = send.at[s]
        copy = pltpu.make_async_remote_copy(
            src_ref=source,
            dst_ref=held.at[s],
            send_sem=send_sem.at[s],
            recv_sem=recv_sem.at[s],
            device_id={"stripe": partner},
            device_id_type=MESH,
        )
        copy.start()
        copy.wait()
        total = total + held[s]
    a = total[:fit, :]
    sub = lax.broadcasted_iota(jnp.int32, a.shape, 0)
    lane = lax.broadcasted_iota(jnp.int32, a.shape, 1)
    for k in range(fit):
        row = a[k : k + 1, :]
        row = row / a[k : k + 1, k : k + 1]
        a = jnp.where(sub == k, row, a - a[:, k : k + 1] * row)
    answer = jnp.broadcast_to(a[:, fit : fit + 1], a.shape)
    out_ref[...] = jnp.zeros_like(out_ref)
    out_ref[:fit, :] = answer
    row_ref[...] = jnp.broadcast_to(
        jnp.sum(jnp.where(sub == lane, answer, 0.0), axis=0, keepdims=True), row_ref.shape
    )


def model_kernel(region_rows, bases, taps, coef_ref, ext_ref, exp_ref, mask_ref, rowf_ref, colf_ref, out_ref, band, wide_y, diff):
    rows, cols = out_ref.shape
    tall = exp_ref.shape[0]
    ext_rows, wide = ext_ref.shape
    first = (lax.axis_index("stripe") * rows - 1).astype(jnp.float32)
    v = row_coords(first, tall, region_rows)
    pad_b = rowf_ref.shape[0]
    mats = []
    for t in range(3):
        c = coef_ref[pl.ds(t, pad_b, stride=3), :]
        mats.append(
            lax.dot_general(
                colf_ref[...] * c,
                rowf_ref[...],
                (((0,), (0,)), ((), ())),
                precision=HIGHEST,
                preferred_element_type=jnp.float32,
            )
        )
    for j in range(taps):
        k0, k1, k2 = (jnp.broadcast_to(m[j : j + 1, :], (tall, EDGE)) for m in mats)
        main = k0 + v * k2 + (-(j - HALF) * 2.0 / cols) * k1
        main = pltpu.roll(main, 0, 1, stride=1, stride_axis=0)
        side = pltpu.roll(k1, ext_rows, 1, stride=1, stride_axis=0)
        band[j * tall : (j + 1) * tall, :] = main + side
    ext = ext_ref[...]
    u_wide = col_coords(-float(EDGE), wide, cols)
    both = jnp.concatenate([ext, ext * u_wide, jnp.zeros((EDGE - 2 * ext_rows, wide), jnp.float32)], axis=0)
    high = both.astype(jnp.bfloat16)
    rest = (both - high.astype(jnp.float32)).astype(jnp.bfloat16)
    weights = band[...]
    w_high = weights.astype(jnp.bfloat16)
    w_rest = (weights - w_high.astype(jnp.float32)).astype(jnp.bfloat16)
    dot = functools.partial(jnp.dot, preferred_element_type=jnp.float32)
    wide_y[...] = dot(w_high, high) + (dot(w_high, rest) + dot(w_rest, high))
    u = col_coords(0.0, cols, cols)
    q = [coef_ref[3 * bases + m : 3 * bases + m + 1, 0:1] for m in range(7)]
    terms = background(u, v)
    level = q[0] + q[1] * terms[1] + q[4] * terms[4]
    model = level + (q[2] * terms[2] + q[5] * terms[5]) + u * (q[3] * v + q[6] * terms[5])
    for j in range(taps):
        y = wide_y[j * tall : (j + 1) * tall, :]
        model = model + pltpu.roll(y, wide - (EDGE - HALF) - j, 1)[:, :cols]
    d = mask_ref[...] * (exp_ref[...] - model)
    diff[...] = d
    lane = lax.broadcasted_iota(jnp.int32, (rows, cols), 1)
    mid = diff[1 : rows + 1, :]
    left = jnp.where(lane == 0, 0.0, pltpu.roll(mid, 1, 1))
    right = jnp.where(lane == cols - 1, 0.0, pltpu.roll(mid, cols - 1, 1))
    around = diff[2 : rows + 2, :] + diff[0:rows, :] + right + left
    out_ref[...] = 4.0 * mid - around


def shards(template, exposure, cosmic_mask, stamp_blocks, row_filters, col_filters):
    rows, cols = exposure.shape[1:]
    bases, taps = row_filters.shape
    fit = 3 * bases + 7
    reach = HALF + 1
    stripes = lax.axis_size("stripe")
    region_rows = rows * stripes
    me_exp = lax.axis_index("exp")
    other = lax.ppermute(template, "exp", [(0, 1), (1, 0)])
    is_first = me_exp == 0
    full = jnp.concatenate([jnp.where(is_first, template, other), jnp.where(is_first, other, template)], axis=1)
    own_exp = exposure[0]
    own_mask = cosmic_mask[0].astype(jnp.float32)
    down = [(i, i + 1) for i in range(stripes - 1)]
    up = [(i + 1, i) for i in range(stripes - 1)]
    above = lax.ppermute(jnp.concatenate([full[rows - reach :], own_exp[rows - 1 :], own_mask[rows - 1 :]]), "stripe", down)
    below = lax.ppermute(jnp.concatenate([full[:reach], own_exp[:1], own_mask[:1]]), "stripe", up)
    ext_rows = round_up(rows + 2 * reach, 8)
    ext = jnp.concatenate([above[:reach], full, below[:reach]], axis=0)
    ext = jnp.pad(ext, ((0, ext_rows - ext.shape[0]), (EDGE, EDGE)))
    wide = ext.shape[1]
    tall = round_up(rows + 2, 8)
    spare = jnp.zeros((tall - rows - 2, cols), jnp.float32)
    exp_tall = jnp.concatenate([above[reach : reach + 1], own_exp, below[reach : reach + 1], spare])
    mask_tall = jnp.concatenate([above[reach + 1 :], own_mask, below[reach + 1 :], spare])
    tap = jnp.arange(ext_rows)[None, :] - jnp.arange(rows)[:, None] - 1
    band = jnp.zeros((bases, rows, ext_rows), jnp.float32)
    for i in range(taps):
        band = band + jnp.where((tap == i)[None], row_filters[:, i][:, None, None], 0.0)
    band = band.reshape(bases * rows, ext_rows)
    parity = jnp.repeat((stamp_blocks % 2).astype(jnp.float32), STAMP_W, axis=1)
    pad_b = round_up(bases, 8)
    row_pad = jnp.pad(row_filters, ((0, pad_b - bases), (0, EDGE - taps)))
    col_pad = jnp.pad(col_filters, ((0, pad_b - bases), (0, EDGE - taps)))
    total = round_up(fit + 1, 8)
    vmem = pl.BlockSpec(memory_space=pltpu.VMEM)
    smem = pl.BlockSpec(memory_space=pltpu.SMEM)
    f32 = jnp.float32
    normal = pl.pallas_call(
        functools.partial(normal_kernel, float(region_rows)),
        out_shape=jax.ShapeDtypeStruct((total, EDGE), f32),
        in_specs=[vmem] * 5 + [smem],
        out_specs=vmem,
        scratch_shapes=[pltpu.VMEM((bases * rows, wide), f32), pltpu.VMEM((cols // (2 * EDGE), total * rows, EDGE), f32)],
        name="normal",
    )(band, ext, own_exp, cosmic_mask[0], parity, col_filters)
    hops = max(1, (stripes - 1).bit_length())
    coef, coef_row = pl.pallas_call(
        functools.partial(solve_kernel, stripes, fit),
        out_shape=(jax.ShapeDtypeStruct((total, EDGE), f32), jax.ShapeDtypeStruct((8, EDGE), f32)),
        in_specs=[vmem],
        out_specs=(vmem, vmem),
        scratch_shapes=[
            pltpu.VMEM((hops, total, EDGE), f32),
            pltpu.VMEM((hops, total, EDGE), f32),
            pltpu.SemaphoreType.DMA((hops,)),
            pltpu.SemaphoreType.DMA((hops,)),
        ],
        compiler_params=pltpu.CompilerParams(collective_id=0, has_side_effects=True),
        name="solve",
    )(normal)
    filtered = pl.pallas_call(
        functools.partial(model_kernel, float(region_rows), bases, taps),
        out_shape=jax.ShapeDtypeStruct((rows, cols), f32),
        in_specs=[vmem] * 6,
        out_specs=vmem,
        scratch_shapes=[
            pltpu.VMEM((taps * tall, EDGE), f32),
            pltpu.VMEM((taps * tall, wide), f32),
            pltpu.VMEM((tall, cols), f32),
        ],
        name="model",
    )(coef, ext, exp_tall, mask_tall, row_pad, col_pad)
    return (filtered[None], coef_row[:1, :fit])


def solution(mesh):
    placed = (
        P(("groups", "stripe"), "exp"),
        P(("groups", "exp"), "stripe", None),
        P(("groups", "exp"), "stripe", None),
        P(("groups", "stripe"), None),
        P(),
        P(),
    )
    return jax.shard_map(
        shards,
        mesh=mesh,
        in_specs=placed,
        out_specs=(P(("groups", "exp"), "stripe", None), P(("groups", "exp"), None)),
        check_vma=False,
    )
```

```python
import functools

import jax
import jax.numpy as jnp
from jax import lax
from jax.experimental import pallas as pl
from jax.experimental.pallas import tpu as pltpu
from jax.sharding import PartitionSpec as P

HALF = 9
STAMP_W = 64
EDGE = 128
HIGHEST = lax.Precision.HIGHEST
MESH = pl.DeviceIdType.MESH


def round_up(n, m):
    return -(-n // m) * m


def row_coords(first, count, region_rows):
    index = lax.broadcasted_iota(jnp.int32, (count, 1), 0).astype(jnp.float32) + first
    return (2.0 * index + 1.0) / region_rows - 1.0


def col_coords(first, count, col_total):
    index = lax.broadcasted_iota(jnp.int32, (1, count), 1).astype(jnp.float32) + first
    return (2.0 * index + 1.0) / col_total - 1.0


def background(u, v):
    uu = 0.5 * (3.0 * u * u - 1.0)
    vv = 0.5 * (3.0 * v * v - 1.0)
    return [None, u, v, u * v, uu, vv, u * vv]


def split(x):
    high = x.astype(jnp.bfloat16)
    return high, (x - high.astype(jnp.float32)).astype(jnp.bfloat16)


def shifted_rows(row, count, start):
    return pltpu.roll(jnp.broadcast_to(row, (count, EDGE)), start, 1, stride=1, stride_axis=0)


def normal_kernel(region_rows, ext_ref, exp_ref, mask_ref, blk_ref, rowf_ref, colf_ref, out_ref, bandw, vert, design):
    bases, taps = rowf_ref.shape
    rows, cols = exp_ref.shape
    ext_rows = ext_ref.shape[0]
    fit = 3 * bases + 7
    total = out_ref.shape[0]
    half_cols = cols // 2
    blocks = half_cols // EDGE
    stamps = 2 * blocks
    low = lax.broadcasted_iota(jnp.int32, (1, EDGE), 1) < STAMP_W
    parity = [blk_ref[0, s] % 2 == 1 for s in range(stamps)]
    lanes = jnp.zeros((1, EDGE - taps), jnp.float32)

    windows = []
    for s in range(stamps):
        part = ext_ref[:, s * EDGE : (s + 3) * EDGE]
        early = pltpu.roll(part, 2 * EDGE + HALF, 1)[:, :EDGE]
        late = pltpu.roll(part, 2 * EDGE + HALF - STAMP_W, 1)[:, :EDGE]
        windows.append(jnp.where(parity[s], late, early))
    window = jnp.concatenate(windows, axis=1)
    w_high, w_rest = split(window)
    gap = jnp.zeros((EDGE - 2 * ext_rows, window.shape[1]), jnp.bfloat16)
    gap2 = jnp.zeros((EDGE - ext_rows, window.shape[1]), jnp.bfloat16)
    stacked = jnp.concatenate([w_high, w_rest, gap, w_high, gap2], axis=0)
    start = ext_rows // 2 - rows // 2 - HALF
    for b in range(bases):
        row = jnp.concatenate([rowf_ref[b : b + 1, :], lanes], axis=1)
        high = row.astype(jnp.bfloat16).astype(jnp.float32)
        twice = shifted_rows(high, rows, start) + shifted_rows(high, rows, start + ext_rows)
        rest = shifted_rows(row - high, rows, start)
        bandw[b * rows : (b + 1) * rows, :] = jnp.concatenate([twice, rest], axis=1)
    vert[...] = jnp.dot(bandw[...].astype(jnp.bfloat16), stacked, preferred_element_type=jnp.float32)

    def pick(x):
        parts = []
        for m in range(blocks):
            a = x[:, 2 * m * EDGE : (2 * m + 1) * EDGE]
            b = x[:, (2 * m + 1) * EDGE : (2 * m + 2) * EDGE]
            a = jnp.where(parity[2 * m], pltpu.roll(a, STAMP_W, 1), a)
            b = jnp.where(parity[2 * m + 1], b, pltpu.roll(b, STAMP_W, 1))
            parts.append(jnp.where(low, a, b))
        return jnp.concatenate(parts, axis=1)

    first = (lax.axis_index("stripe") * rows).astype(jnp.float32)
    v = jnp.broadcast_to(row_coords(first, rows, region_rows), (rows, half_cols))
    u_all = jnp.broadcast_to(col_coords(0.0, cols, cols), (8, cols))
    u = jnp.broadcast_to(pick(u_all)[0:1], (rows, half_cols))
    good = pick(mask_ref[...].astype(jnp.float32))

    def put(n, x):
        x = x * good
        for m in range(blocks):
            design[m, n * rows : (n + 1) * rows, :] = x[:, m * EDGE : (m + 1) * EDGE]

    for b in range(bases):
        x = vert[b * rows : (b + 1) * rows, :]
        x = jnp.concatenate([x[:, s * EDGE : (s + 1) * EDGE] for s in range(stamps)], axis=0)
        x_high, x_rest = split(x)
        row = jnp.concatenate([colf_ref[b : b + 1, :], lanes], axis=1)
        t_high, t_rest = split(shifted_rows(row, STAMP_W, 0))
        upper = jnp.concatenate([t_high, t_high], axis=1)
        lower = jnp.concatenate([t_rest, jnp.zeros_like(t_rest)], axis=1)
        y = lax.dot_general(
            jnp.concatenate([x_high, x_rest], axis=1),
            jnp.concatenate([upper, lower], axis=0),
            (((1,), (1,)), ((), ())),
            preferred_element_type=jnp.float32,
        )
        y = y + pltpu.roll(y, STAMP_W, 1)
        picked = jnp.concatenate(
            [
                jnp.where(low, y[2 * m * rows : (2 * m + 1) * rows], y[(2 * m + 1) * rows : (2 * m + 2) * rows])
                for m in range(blocks)
            ],
            axis=1,
        )
        put(3 * b, picked)
        put(3 * b + 1, picked * u)
        put(3 * b + 2, picked * v)

    terms = background(u, v)
    terms[0] = jnp.ones_like(u)
    for m, term in enumerate(terms):
        put(3 * bases + m, term)
    put(fit, pick(exp_ref[...]))
    for n in range(fit + 1, total):
        put(n, jnp.zeros_like(u))
    acc = jnp.zeros((total, total), jnp.float32)
    for r in range(rows):
        x = [design[m, pl.ds(r, total, stride=rows), :] for m in range(blocks)]
        x = jnp.concatenate(x, axis=1).astype(jnp.bfloat16)
        acc = acc + lax.dot_general(x, x, (((1,), (1,)), ((), ())), preferred_element_type=jnp.float32)
    out_ref[...] = jnp.concatenate([acc, jnp.zeros((total, EDGE - total), jnp.float32)], axis=1)


def solve_kernel(count, fit, local_ref, out_ref, send, held, send_sem, recv_sem):
    me = lax.axis_index("stripe")
    steps = []
    d = 1
    while d < count:
        steps.append(d)
        d *= 2
    partners = [me + d * (1 - 2 * ((me // d) % 2)) for d in steps]
    barrier = pltpu.get_barrier_semaphore()
    for partner in partners:
        pl.semaphore_signal(barrier, inc=1, device_id={"stripe": partner}, device_id_type=MESH)
    pl.semaphore_wait(barrier, len(partners))
    total = local_ref[...]
    for s, partner in enumerate(partners):
        source = local_ref
        if s:
            send[s] = total
            source = send.at[s]
        copy = pltpu.make_async_remote_copy(
            src_ref=source,
            dst_ref=held.at[s],
            send_sem=send_sem.at[s],
            recv_sem=recv_sem.at[s],
            device_id={"stripe": partner},
            device_id_type=MESH,
        )
        copy.start()
        copy.wait()
        total = total + held[s]
    a = total[:fit, :]
    sub = lax.broadcasted_iota(jnp.int32, a.shape, 0)
    for k in range(fit):
        row = a[k : k + 1, :]
        row = row * pl.reciprocal(jnp.broadcast_to(a[k : k + 1, k : k + 1], row.shape))
        a = jnp.where(sub == k, row, a - a[:, k : k + 1] * row)
    answer = jnp.broadcast_to(a[:, fit : fit + 1], a.shape)
    out_ref[...] = jnp.zeros_like(out_ref)
    out_ref[:fit, :] = answer


def model_kernel(region_rows, coef_ref, ext_ref, exp_ref, mask_ref, rowf_ref, colf_ref, out_ref, row_ref, band, wide_y, diff):
    rows, cols = out_ref.shape
    bases, taps = rowf_ref.shape
    fit = 3 * bases + 7
    tall = exp_ref.shape[0]
    answer = coef_ref[:fit, :fit]
    same = lax.broadcasted_iota(jnp.int32, (fit, fit), 0) == lax.broadcasted_iota(jnp.int32, (fit, fit), 1)
    row_ref[...] = jnp.sum(jnp.where(same, answer, 0.0), axis=0, keepdims=True)
    ext_rows, wide = ext_ref.shape
    first = (lax.axis_index("stripe") * rows - 1).astype(jnp.float32)
    v = row_coords(first, tall, region_rows)
    rowf = jnp.concatenate([rowf_ref[...], jnp.zeros((bases, EDGE - taps), jnp.float32)], axis=1)
    colf = jnp.concatenate([colf_ref[...], jnp.zeros((bases, EDGE - taps), jnp.float32)], axis=1)
    start = ext_rows // 2 - rows // 2 - HALF - 1
    mats = []
    for t in range(3):
        c = coef_ref[pl.ds(t, bases, stride=3), :]
        mats.append(
            lax.dot_general(
                colf * c,
                rowf,
                (((0,), (0,)), ((), ())),
                precision=HIGHEST,
                preferred_element_type=jnp.float32,
            )
        )
    for j in range(taps):
        k0, k1, k2 = (jnp.broadcast_to(m[j : j + 1, :], (tall, EDGE)) for m in mats)
        main = k0 + v * k2 + (-(j - HALF) * 2.0 / cols) * k1
        main = shifted_rows(main, tall, start)
        side = shifted_rows(k1, tall, start + ext_rows)
        band[j * tall : (j + 1) * tall, :] = main + side
    ext = ext_ref[...]
    u_wide = col_coords(-float(EDGE), wide, cols)
    both = jnp.concatenate([ext, ext * u_wide, jnp.zeros((EDGE - 2 * ext_rows, wide), jnp.float32)], axis=0)
    high, rest = split(both)
    w_high, w_rest = split(band[...])
    dot = functools.partial(jnp.dot, preferred_element_type=jnp.float32)
    wide_y[...] = dot(w_high, high) + (dot(w_high, rest) + dot(w_rest, high))
    u = col_coords(0.0, cols, cols)
    q = [coef_ref[3 * bases + m : 3 * bases + m + 1, 0:1] for m in range(7)]
    terms = background(u, v)
    level = q[0] + q[1] * terms[1] + q[4] * terms[4]
    model = level + (q[2] * terms[2] + q[5] * terms[5]) + u * (q[3] * v + q[6] * terms[5])
    for j in range(taps):
        y = wide_y[j * tall : (j + 1) * tall, :]
        model = model + pltpu.roll(y, wide - (EDGE - HALF) - j, 1)[:, :cols]
    d = mask_ref[...] * (exp_ref[...] - model)
    diff[...] = d
    lane = lax.broadcasted_iota(jnp.int32, (rows, cols), 1)
    mid = diff[1 : rows + 1, :]
    left = jnp.where(lane == 0, 0.0, pltpu.roll(mid, 1, 1))
    right = jnp.where(lane == cols - 1, 0.0, pltpu.roll(mid, cols - 1, 1))
    around = diff[2 : rows + 2, :] + diff[0:rows, :] + right + left
    out_ref[...] = 4.0 * mid - around


def shards(template, exposure, cosmic_mask, stamp_blocks, row_filters, col_filters):
    rows, cols = exposure.shape[1:]
    bases, taps = row_filters.shape
    fit = 3 * bases + 7
    reach = HALF + 1
    stripes = lax.axis_size("stripe")
    region_rows = rows * stripes
    me_exp = lax.axis_index("exp")
    other = lax.ppermute(template, "exp", [(0, 1), (1, 0)])
    is_first = me_exp == 0
    full = jnp.concatenate([jnp.where(is_first, template, other), jnp.where(is_first, other, template)], axis=1)
    own_exp = exposure[0]
    own_mask = cosmic_mask[0].astype(jnp.float32)
    down = [(i, i + 1) for i in range(stripes - 1)]
    up = [(i + 1, i) for i in range(stripes - 1)]
    above = lax.ppermute(jnp.concatenate([full[rows - reach :], own_exp[rows - 1 :], own_mask[rows - 1 :]]), "stripe", down)
    below = lax.ppermute(jnp.concatenate([full[:reach], own_exp[:1], own_mask[:1]]), "stripe", up)
    side = round_up(reach, 16)
    ext_rows = rows + 2 * side
    ext = jnp.concatenate([above[:reach], full, below[:reach]], axis=0)
    ext = jnp.pad(ext, ((side - reach, side - reach), (EDGE, EDGE)))
    wide = ext.shape[1]
    tall = round_up(rows + 2, 8)
    spare = jnp.zeros((tall - rows - 2, cols), jnp.float32)
    exp_tall = jnp.concatenate([above[reach : reach + 1], own_exp, below[reach : reach + 1], spare])
    mask_tall = jnp.concatenate([above[reach + 1 :], own_mask, below[reach + 1 :], spare])
    total = round_up(fit + 1, 8)
    vmem = pl.BlockSpec(memory_space=pltpu.VMEM)
    smem = pl.BlockSpec(memory_space=pltpu.SMEM)
    f32 = jnp.float32
    normal = pl.pallas_call(
        functools.partial(normal_kernel, float(region_rows)),
        out_shape=jax.ShapeDtypeStruct((total, EDGE), f32),
        in_specs=[vmem] * 3 + [smem] + [vmem] * 2,
        out_specs=vmem,
        scratch_shapes=[
            pltpu.VMEM((bases * rows, 2 * EDGE), f32),
            pltpu.VMEM((bases * rows, cols), f32),
            pltpu.VMEM((cols // (2 * EDGE), total * rows, EDGE), f32),
        ],
        name="normal",
    )(ext, own_exp, cosmic_mask[0], stamp_blocks, row_filters, col_filters)
    hops = max(1, (stripes - 1).bit_length())
    coef = pl.pallas_call(
        functools.partial(solve_kernel, stripes, fit),
        out_shape=jax.ShapeDtypeStruct((total, EDGE), f32),
        in_specs=[vmem],
        out_specs=vmem,
        scratch_shapes=[
            pltpu.VMEM((hops, total, EDGE), f32),
            pltpu.VMEM((hops, total, EDGE), f32),
            pltpu.SemaphoreType.DMA((hops,)),
            pltpu.SemaphoreType.DMA((hops,)),
        ],
        compiler_params=pltpu.CompilerParams(collective_id=0, has_side_effects=True),
        name="solve",
    )(normal)
    filtered, coef_row = pl.pallas_call(
        functools.partial(model_kernel, float(region_rows)),
        out_shape=(jax.ShapeDtypeStruct((rows, cols), f32), jax.ShapeDtypeStruct((1, fit), f32)),
        in_specs=[vmem] * 6,
        out_specs=(vmem, vmem),
        scratch_shapes=[
            pltpu.VMEM((taps * tall, EDGE), f32),
            pltpu.VMEM((taps * tall, wide), f32),
            pltpu.VMEM((tall, cols), f32),
        ],
        name="model",
    )(coef, ext, exp_tall, mask_tall, row_filters, col_filters)
    return (filtered[None], coef_row)


def solution(mesh):
    placed = (
        P(("groups", "stripe"), "exp"),
        P(("groups", "exp"), "stripe", None),
        P(("groups", "exp"), "stripe", None),
        P(("groups", "stripe"), None),
        P(),
        P(),
    )
    return jax.shard_map(
        shards,
        mesh=mesh,
        in_specs=placed,
        out_specs=(P(("groups", "exp"), "stripe", None), P(("groups", "exp"), None)),
        check_vma=False,
    )
```

```python
import functools

import jax
import jax.numpy as jnp
from jax import lax
from jax.experimental import pallas as pl
from jax.experimental.pallas import tpu as pltpu
from jax.sharding import PartitionSpec as P

HALF = 9
STAMP_W = 64
EDGE = 128
HIGHEST = lax.Precision.HIGHEST
MESH = pl.DeviceIdType.MESH


def round_up(n, m):
    return -(-n // m) * m


def row_coords(first, count, region_rows):
    index = lax.broadcasted_iota(jnp.int32, (count, 1), 0).astype(jnp.float32) + first
    return (2.0 * index + 1.0) / region_rows - 1.0


def col_coords(first, count, col_total):
    index = lax.broadcasted_iota(jnp.int32, (1, count), 1).astype(jnp.float32) + first
    return (2.0 * index + 1.0) / col_total - 1.0


def background(u, v):
    uu = 0.5 * (3.0 * u * u - 1.0)
    vv = 0.5 * (3.0 * v * v - 1.0)
    return [None, u, v, u * v, uu, vv, u * vv]


def split(x):
    high = x.astype(jnp.bfloat16)
    return high, (x - high.astype(jnp.float32)).astype(jnp.bfloat16)


def shifted_rows(row, count, start):
    return pltpu.roll(jnp.broadcast_to(row, (count, EDGE)), start, 1, stride=1, stride_axis=0)


def normal_kernel(region_rows, ext_ref, exp_ref, mask_ref, blk_ref, rowf_ref, colf_ref, out_ref, bandw, vert, design):
    bases, taps = rowf_ref.shape
    rows, cols = exp_ref.shape
    ext_rows = ext_ref.shape[0]
    fit = 3 * bases + 7
    total = out_ref.shape[0]
    half_cols = cols // 2
    blocks = half_cols // EDGE
    stamps = 2 * blocks
    low = lax.broadcasted_iota(jnp.int32, (1, EDGE), 1) < STAMP_W
    parity = [blk_ref[0, s] % 2 == 1 for s in range(stamps)]
    lanes = jnp.zeros((1, EDGE - taps), jnp.float32)

    windows = []
    for s in range(stamps):
        part = ext_ref[:, s * EDGE : (s + 3) * EDGE]
        early = pltpu.roll(part, 2 * EDGE + HALF, 1)[:, :EDGE]
        late = pltpu.roll(part, 2 * EDGE + HALF - STAMP_W, 1)[:, :EDGE]
        windows.append(jnp.where(parity[s], late, early))
    window = jnp.concatenate(windows, axis=1)
    w_high, w_rest = split(window)
    gap = jnp.zeros((EDGE - 2 * ext_rows, window.shape[1]), jnp.bfloat16)
    gap2 = jnp.zeros((EDGE - ext_rows, window.shape[1]), jnp.bfloat16)
    stacked = jnp.concatenate([w_high, w_rest, gap, w_high, gap2], axis=0)
    start = ext_rows // 2 - rows // 2 - HALF
    for b in range(bases):
        row = jnp.concatenate([rowf_ref[b : b + 1, :], lanes], axis=1)
        high = row.astype(jnp.bfloat16).astype(jnp.float32)
        twice = shifted_rows(high, rows, start) + shifted_rows(high, rows, start + ext_rows)
        rest = shifted_rows(row - high, rows, start)
        bandw[b * rows : (b + 1) * rows, :] = jnp.concatenate([twice, rest], axis=1)
    vert[...] = jnp.dot(bandw[...].astype(jnp.bfloat16), stacked, preferred_element_type=jnp.float32)

    def pick(x):
        parts = []
        for m in range(blocks):
            a = x[:, 2 * m * EDGE : (2 * m + 1) * EDGE]
            b = x[:, (2 * m + 1) * EDGE : (2 * m + 2) * EDGE]
            a = jnp.where(parity[2 * m], pltpu.roll(a, STAMP_W, 1), a)
            b = jnp.where(parity[2 * m + 1], b, pltpu.roll(b, STAMP_W, 1))
            parts.append(jnp.where(low, a, b))
        return jnp.concatenate(parts, axis=1)

    first = (lax.axis_index("stripe") * rows).astype(jnp.float32)
    v = jnp.broadcast_to(row_coords(first, rows, region_rows), (rows, half_cols))
    u_all = jnp.broadcast_to(col_coords(0.0, cols, cols), (8, cols))
    u = jnp.broadcast_to(pick(u_all)[0:1], (rows, half_cols))
    good = pick(mask_ref[...].astype(jnp.float32))

    def put(n, x):
        x = x * good
        for m in range(blocks):
            design[m, n * rows : (n + 1) * rows, :] = x[:, m * EDGE : (m + 1) * EDGE]

    for b in range(bases):
        x = vert[b * rows : (b + 1) * rows, :]
        x = jnp.concatenate([x[:, s * EDGE : (s + 1) * EDGE] for s in range(stamps)], axis=0)
        x_high, x_rest = split(x)
        row = jnp.concatenate([colf_ref[b : b + 1, :], lanes], axis=1)
        t_high, t_rest = split(shifted_rows(row, STAMP_W, 0))
        upper = jnp.concatenate([t_high, t_high], axis=1)
        lower = jnp.concatenate([t_rest, jnp.zeros_like(t_rest)], axis=1)
        y = lax.dot_general(
            jnp.concatenate([x_high, x_rest], axis=1),
            jnp.concatenate([upper, lower], axis=0),
            (((1,), (1,)), ((), ())),
            preferred_element_type=jnp.float32,
        )
        y = y + pltpu.roll(y, STAMP_W, 1)
        picked = jnp.concatenate(
            [
                jnp.where(low, y[2 * m * rows : (2 * m + 1) * rows], y[(2 * m + 1) * rows : (2 * m + 2) * rows])
                for m in range(blocks)
            ],
            axis=1,
        )
        put(3 * b, picked)
        put(3 * b + 1, picked * u)
        put(3 * b + 2, picked * v)

    terms = background(u, v)
    terms[0] = jnp.ones_like(u)
    for m, term in enumerate(terms):
        put(3 * bases + m, term)
    put(fit, pick(exp_ref[...]))
    for n in range(fit + 1, total):
        put(n, jnp.zeros_like(u))
    acc = jnp.zeros((total, total), jnp.float32)
    for r in range(rows):
        x = [design[m, pl.ds(r, total, stride=rows), :] for m in range(blocks)]
        x = jnp.concatenate(x, axis=1).astype(jnp.bfloat16)
        acc = acc + lax.dot_general(x, x, (((1,), (1,)), ((), ())), preferred_element_type=jnp.float32)
    out_ref[...] = jnp.concatenate([acc, jnp.zeros((total, EDGE - total), jnp.float32)], axis=1)


def solve_kernel(count, fit, local_ref, out_ref, send, held, send_sem, recv_sem):
    me = lax.axis_index("stripe")
    steps = []
    d = 1
    while d < count:
        steps.append(d)
        d *= 2
    partners = [me + d * (1 - 2 * ((me // d) % 2)) for d in steps]
    barrier = pltpu.get_barrier_semaphore()
    for partner in partners:
        pl.semaphore_signal(barrier, inc=1, device_id={"stripe": partner}, device_id_type=MESH)
    pl.semaphore_wait(barrier, len(partners))
    total = local_ref[...]
    for s, partner in enumerate(partners):
        source = local_ref
        if s:
            send[s] = total
            source = send.at[s]
        copy = pltpu.make_async_remote_copy(
            src_ref=source,
            dst_ref=held.at[s],
            send_sem=send_sem.at[s],
            recv_sem=recv_sem.at[s],
            device_id={"stripe": partner},
            device_id_type=MESH,
        )
        copy.start()
        copy.wait()
        total = total + held[s]
    a = total[:fit, :]
    sub = lax.broadcasted_iota(jnp.int32, a.shape, 0)
    for k in range(fit):
        row = a[k : k + 1, :]
        row = row * pl.reciprocal(jnp.broadcast_to(a[k : k + 1, k : k + 1], row.shape))
        a = jnp.where(sub == k, row, a - a[:, k : k + 1] * row)
    answer = jnp.broadcast_to(a[:, fit : fit + 1], a.shape)
    out_ref[...] = jnp.zeros_like(out_ref)
    out_ref[:fit, :] = answer


def model_kernel(region_rows, coef_ref, ext_ref, exp_ref, mask_ref, edge_ref, rowf_ref, colf_ref, out_ref, row_ref, band, wide_y, diff):
    rows, cols = out_ref.shape
    bases, taps = rowf_ref.shape
    fit = 3 * bases + 7
    tall = diff.shape[0]
    answer = coef_ref[:fit, :fit]
    same = lax.broadcasted_iota(jnp.int32, (fit, fit), 0) == lax.broadcasted_iota(jnp.int32, (fit, fit), 1)
    row_ref[...] = jnp.sum(jnp.where(same, answer, 0.0), axis=0, keepdims=True)
    ext_rows, wide = ext_ref.shape
    first = (lax.axis_index("stripe") * rows - 1).astype(jnp.float32)
    v = row_coords(first, tall, region_rows)
    rowf = jnp.concatenate([rowf_ref[...], jnp.zeros((bases, EDGE - taps), jnp.float32)], axis=1)
    colf = jnp.concatenate([colf_ref[...], jnp.zeros((bases, EDGE - taps), jnp.float32)], axis=1)
    start = ext_rows // 2 - rows // 2 - HALF - 1
    mats = []
    for t in range(3):
        c = coef_ref[pl.ds(t, bases, stride=3), :]
        mats.append(
            lax.dot_general(
                colf * c,
                rowf,
                (((0,), (0,)), ((), ())),
                precision=HIGHEST,
                preferred_element_type=jnp.float32,
            )
        )
    for j in range(taps):
        k0, k1, k2 = (jnp.broadcast_to(m[j : j + 1, :], (tall, EDGE)) for m in mats)
        main = k0 + v * k2 + (-(j - HALF) * 2.0 / cols) * k1
        main = shifted_rows(main, tall, start)
        side = shifted_rows(k1, tall, start + ext_rows)
        band[j * tall : (j + 1) * tall, :] = main + side
    ext = ext_ref[...]
    u_wide = col_coords(-float(EDGE), wide, cols)
    both = jnp.concatenate([ext, ext * u_wide, jnp.zeros((EDGE - 2 * ext_rows, wide), jnp.float32)], axis=0)
    high, rest = split(both)
    w_high, w_rest = split(band[...])
    dot = functools.partial(jnp.dot, preferred_element_type=jnp.float32)
    wide_y[...] = dot(w_high, high) + (dot(w_high, rest) + dot(w_rest, high))
    u = col_coords(0.0, cols, cols)
    q = [coef_ref[3 * bases + m : 3 * bases + m + 1, 0:1] for m in range(7)]
    terms = background(u, v)
    level = q[0] + q[1] * terms[1] + q[4] * terms[4]
    model = level + (q[2] * terms[2] + q[5] * terms[5]) + u * (q[3] * v + q[6] * terms[5])
    for j in range(taps):
        y = wide_y[j * tall : (j + 1) * tall, :]
        model = model + pltpu.roll(y, wide - (EDGE - HALF) - j, 1)[:, :cols]
    spare = jnp.zeros((tall - rows - 2, cols), jnp.float32)
    science = jnp.concatenate([edge_ref[0, 0:1, :], exp_ref[...], edge_ref[1, 0:1, :], spare], axis=0)
    good = jnp.concatenate(
        [edge_ref[0, 1:2, :], mask_ref[...].astype(jnp.float32), edge_ref[1, 1:2, :], spare], axis=0
    )
    diff[...] = good * (science - model)
    lane = lax.broadcasted_iota(jnp.int32, (rows, cols), 1)
    mid = diff[1 : rows + 1, :]
    left = jnp.where(lane == 0, 0.0, pltpu.roll(mid, 1, 1))
    right = jnp.where(lane == cols - 1, 0.0, pltpu.roll(mid, cols - 1, 1))
    around = diff[2 : rows + 2, :] + diff[0:rows, :] + right + left
    out_ref[...] = 4.0 * mid - around


def halo_kernel(count, tmpl_ref, exp_ref, mask_ref, ext_ref, edge_ref, parts, edge_send, edge_recv, send_sem, recv_sem):
    me = lax.axis_index("stripe")
    core = lax.axis_index("exp")
    rows, half = tmpl_ref.shape
    has_up = me > 0
    has_down = me < count - 1

    def copy(src, dst, n, stripe, exp):
        return pltpu.make_async_remote_copy(
            src_ref=src,
            dst_ref=dst,
            send_sem=send_sem.at[n],
            recv_sem=recv_sem.at[n],
            device_id={"stripe": stripe, "exp": exp},
            device_id_type=MESH,
        )

    def downs():
        return [
            copy(edge_send.at[0], edge_recv.at[0], 2, me + 1, core),
            copy(tmpl_ref, parts.at[0], 0, me + 1, core),
            copy(tmpl_ref, parts.at[1], 1, me + 1, 1 - core),
        ]

    def ups():
        return [
            copy(edge_send.at[1], edge_recv.at[1], 5, me - 1, core),
            copy(tmpl_ref, parts.at[2], 3, me - 1, core),
            copy(tmpl_ref, parts.at[3], 4, me - 1, 1 - core),
        ]

    edge_send[0, 0:1, :] = exp_ref[rows - 1 : rows, :]
    edge_send[0, 1:2, :] = mask_ref[rows - 1 : rows, :].astype(jnp.float32)
    edge_send[1, 0:1, :] = exp_ref[0:1, :]
    edge_send[1, 1:2, :] = mask_ref[0:1, :].astype(jnp.float32)
    barrier = pltpu.get_barrier_semaphore()

    def greet(stripe, exp):
        pl.semaphore_signal(barrier, inc=1, device_id={"stripe": stripe, "exp": exp}, device_id_type=MESH)

    @pl.when(has_up)
    def _():
        greet(me - 1, core)
        greet(me - 1, 1 - core)

    @pl.when(has_down)
    def _():
        greet(me + 1, core)
        greet(me + 1, 1 - core)

    greet(me, 1 - core)
    pl.semaphore_wait(barrier, 1 + 2 * has_up.astype(jnp.int32) + 2 * has_down.astype(jnp.int32))

    @pl.when(has_down)
    def _():
        for c in downs():
            c.start()

    @pl.when(has_up)
    def _():
        for c in ups():
            c.start()

    across = copy(tmpl_ref, parts.at[4], 6, me, 1 - core)
    across.start()
    ext_ref[...] = jnp.zeros_like(ext_ref)
    edge_ref[...] = jnp.zeros_like(edge_ref)
    mine = pl.ds(pl.multiple_of(EDGE + core * half, EDGE), half)
    theirs = pl.ds(pl.multiple_of(EDGE + (1 - core) * half, EDGE), half)
    ext_ref[rows : 2 * rows, mine] = tmpl_ref[...]
    across.wait()
    ext_ref[rows : 2 * rows, theirs] = parts[4]

    @pl.when(has_up)
    def _():
        for c in downs():
            c.wait_recv()
        edge_ref[0] = edge_recv[0]
        ext_ref[0:rows, mine] = parts[0]
        ext_ref[0:rows, theirs] = parts[1]

    @pl.when(has_down)
    def _():
        for c in ups():
            c.wait_recv()
        edge_ref[1] = edge_recv[1]
        ext_ref[2 * rows : 3 * rows, mine] = parts[2]
        ext_ref[2 * rows : 3 * rows, theirs] = parts[3]

    @pl.when(has_down)
    def _():
        for c in downs():
            c.wait_send()

    @pl.when(has_up)
    def _():
        for c in ups():
            c.wait_send()


def shards(template, exposure, cosmic_mask, stamp_blocks, row_filters, col_filters):
    rows, cols = exposure.shape[1:]
    bases, taps = row_filters.shape
    fit = 3 * bases + 7
    stripes = lax.axis_size("stripe")
    region_rows = rows * stripes
    own_exp = exposure[0]
    own_mask = cosmic_mask[0]
    half = template.shape[1]
    ext_rows = 3 * rows
    wide = cols + 2 * EDGE
    tall = round_up(rows + 2, 8)
    total = round_up(fit + 1, 8)
    vmem = pl.BlockSpec(memory_space=pltpu.VMEM)
    smem = pl.BlockSpec(memory_space=pltpu.SMEM)
    f32 = jnp.float32
    ext, edges = pl.pallas_call(
        functools.partial(halo_kernel, stripes),
        out_shape=(jax.ShapeDtypeStruct((ext_rows, wide), f32), jax.ShapeDtypeStruct((2, 2, cols), f32)),
        in_specs=[vmem] * 3,
        out_specs=(vmem, vmem),
        scratch_shapes=[
            pltpu.VMEM((5, rows, half), f32),
            pltpu.VMEM((2, 2, cols), f32),
            pltpu.VMEM((2, 2, cols), f32),
            pltpu.SemaphoreType.DMA((7,)),
            pltpu.SemaphoreType.DMA((7,)),
        ],
        compiler_params=pltpu.CompilerParams(collective_id=1, has_side_effects=True),
        name="halo",
    )(template, own_exp, own_mask)
    normal = pl.pallas_call(
        functools.partial(normal_kernel, float(region_rows)),
        out_shape=jax.ShapeDtypeStruct((total, EDGE), f32),
        in_specs=[vmem] * 3 + [smem] + [vmem] * 2,
        out_specs=vmem,
        scratch_shapes=[
            pltpu.VMEM((bases * rows, 2 * EDGE), f32),
            pltpu.VMEM((bases * rows, cols), f32),
            pltpu.VMEM((cols // (2 * EDGE), total * rows, EDGE), f32),
        ],
        name="normal",
    )(ext, own_exp, own_mask, stamp_blocks, row_filters, col_filters)
    hops = max(1, (stripes - 1).bit_length())
    coef = pl.pallas_call(
        functools.partial(solve_kernel, stripes, fit),
        out_shape=jax.ShapeDtypeStruct((total, EDGE), f32),
        in_specs=[vmem],
        out_specs=vmem,
        scratch_shapes=[
            pltpu.VMEM((hops, total, EDGE), f32),
            pltpu.VMEM((hops, total, EDGE), f32),
            pltpu.SemaphoreType.DMA((hops,)),
            pltpu.SemaphoreType.DMA((hops,)),
        ],
        compiler_params=pltpu.CompilerParams(collective_id=0, has_side_effects=True),
        name="solve",
    )(normal)
    filtered, coef_row = pl.pallas_call(
        functools.partial(model_kernel, float(region_rows)),
        out_shape=(jax.ShapeDtypeStruct((rows, cols), f32), jax.ShapeDtypeStruct((1, fit), f32)),
        in_specs=[vmem] * 7,
        out_specs=(vmem, vmem),
        scratch_shapes=[
            pltpu.VMEM((taps * tall, EDGE), f32),
            pltpu.VMEM((taps * tall, wide), f32),
            pltpu.VMEM((tall, cols), f32),
        ],
        name="model",
    )(coef, ext, own_exp, own_mask, edges, row_filters, col_filters)
    return (filtered[None], coef_row)


def solution(mesh):
    placed = (
        P(("groups", "stripe"), "exp"),
        P(("groups", "exp"), "stripe", None),
        P(("groups", "exp"), "stripe", None),
        P(("groups", "stripe"), None),
        P(),
        P(),
    )
    return jax.shard_map(
        shards,
        mesh=mesh,
        in_specs=placed,
        out_specs=(P(("groups", "exp"), "stripe", None), P(("groups", "exp"), None)),
        check_vma=False,
    )
```

```python
import functools

import jax
import jax.numpy as jnp
from jax import lax
from jax.experimental import pallas as pl
from jax.experimental.pallas import tpu as pltpu
from jax.sharding import PartitionSpec as P

HALF = 9
STAMP_W = 64
EDGE = 128
TILE = 8
BLOCK = 4
HIGHEST = lax.Precision.HIGHEST
MESH = pl.DeviceIdType.MESH


def round_up(n, m):
    return -(-n // m) * m


def row_coords(first, count, region_rows):
    index = lax.broadcasted_iota(jnp.int32, (count, 1), 0).astype(jnp.float32) + first
    return (2.0 * index + 1.0) / region_rows - 1.0


def col_coords(first, count, col_total):
    index = lax.broadcasted_iota(jnp.int32, (1, count), 1).astype(jnp.float32) + first
    return (2.0 * index + 1.0) / col_total - 1.0


def background(u, v):
    uu = 0.5 * (3.0 * u * u - 1.0)
    vv = 0.5 * (3.0 * v * v - 1.0)
    return [None, u, v, u * v, uu, vv, u * vv]


def split(x):
    high = x.astype(jnp.bfloat16)
    return high, (x - high.astype(jnp.float32)).astype(jnp.bfloat16)


def shifted_rows(row, count, start):
    return pltpu.roll(jnp.broadcast_to(row, (count, EDGE)), start, 1, stride=1, stride_axis=0)


def normal_kernel(region_rows, ext_ref, exp_ref, mask_ref, blk_ref, rowf_ref, colf_ref, out_ref, bandw, vert, design):
    bases, taps = rowf_ref.shape
    rows, cols = exp_ref.shape
    ext_rows = ext_ref.shape[0]
    fit = 3 * bases + 7
    total = out_ref.shape[0]
    half_cols = cols // 2
    blocks = half_cols // EDGE
    stamps = 2 * blocks
    low = lax.broadcasted_iota(jnp.int32, (1, EDGE), 1) < STAMP_W
    parity = [blk_ref[0, s] % 2 == 1 for s in range(stamps)]
    lanes = jnp.zeros((1, EDGE - taps), jnp.float32)

    windows = []
    for s in range(stamps):
        part = ext_ref[:, s * EDGE : (s + 3) * EDGE]
        early = pltpu.roll(part, 2 * EDGE + HALF, 1)[:, :EDGE]
        late = pltpu.roll(part, 2 * EDGE + HALF - STAMP_W, 1)[:, :EDGE]
        windows.append(jnp.where(parity[s], late, early))
    window = jnp.concatenate(windows, axis=1)
    w_high, w_rest = split(window)
    gap = jnp.zeros((EDGE - 2 * ext_rows, window.shape[1]), jnp.bfloat16)
    gap2 = jnp.zeros((EDGE - ext_rows, window.shape[1]), jnp.bfloat16)
    stacked = jnp.concatenate([w_high, w_rest, gap, w_high, gap2], axis=0)
    start = ext_rows // 2 - rows // 2 - HALF
    for b in range(bases):
        row = jnp.concatenate([rowf_ref[b : b + 1, :], lanes], axis=1)
        high = row.astype(jnp.bfloat16).astype(jnp.float32)
        twice = shifted_rows(high, rows, start) + shifted_rows(high, rows, start + ext_rows)
        rest = shifted_rows(row - high, rows, start)
        bandw[b * rows : (b + 1) * rows, :] = jnp.concatenate([twice, rest], axis=1)
    vert[...] = jnp.dot(bandw[...].astype(jnp.bfloat16), stacked, preferred_element_type=jnp.float32)

    def pick(x):
        parts = []
        for m in range(blocks):
            a = x[:, 2 * m * EDGE : (2 * m + 1) * EDGE]
            b = x[:, (2 * m + 1) * EDGE : (2 * m + 2) * EDGE]
            a = jnp.where(parity[2 * m], pltpu.roll(a, STAMP_W, 1), a)
            b = jnp.where(parity[2 * m + 1], b, pltpu.roll(b, STAMP_W, 1))
            parts.append(jnp.where(low, a, b))
        return jnp.concatenate(parts, axis=1)

    first = (lax.axis_index("stripe") * rows).astype(jnp.float32)
    v = jnp.broadcast_to(row_coords(first, rows, region_rows), (rows, half_cols))
    u_all = jnp.broadcast_to(col_coords(0.0, cols, cols), (8, cols))
    u = jnp.broadcast_to(pick(u_all)[0:1], (rows, half_cols))
    good = pick(mask_ref[...].astype(jnp.float32))

    def put(n, x):
        x = x * good
        for m in range(blocks):
            design[m, n * rows : (n + 1) * rows, :] = x[:, m * EDGE : (m + 1) * EDGE]

    for b in range(bases):
        x = vert[b * rows : (b + 1) * rows, :]
        x = jnp.concatenate([x[:, s * EDGE : (s + 1) * EDGE] for s in range(stamps)], axis=0)
        x_high, x_rest = split(x)
        row = jnp.concatenate([colf_ref[b : b + 1, :], lanes], axis=1)
        t_high, t_rest = split(shifted_rows(row, STAMP_W, 0))
        upper = jnp.concatenate([t_high, t_high], axis=1)
        lower = jnp.concatenate([t_rest, jnp.zeros_like(t_rest)], axis=1)
        y = lax.dot_general(
            jnp.concatenate([x_high, x_rest], axis=1),
            jnp.concatenate([upper, lower], axis=0),
            (((1,), (1,)), ((), ())),
            preferred_element_type=jnp.float32,
        )
        y = y + pltpu.roll(y, STAMP_W, 1)
        picked = jnp.concatenate(
            [
                jnp.where(low, y[2 * m * rows : (2 * m + 1) * rows], y[(2 * m + 1) * rows : (2 * m + 2) * rows])
                for m in range(blocks)
            ],
            axis=1,
        )
        put(3 * b, picked)
        put(3 * b + 1, picked * u)
        put(3 * b + 2, picked * v)

    terms = background(u, v)
    terms[0] = jnp.ones_like(u)
    for m, term in enumerate(terms):
        put(3 * bases + m, term)
    put(fit, pick(exp_ref[...]))
    for n in range(fit + 1, total):
        put(n, jnp.zeros_like(u))
    acc = jnp.zeros((total, total), jnp.float32)
    for r in range(rows):
        x = [design[m, pl.ds(r, total, stride=rows), :] for m in range(blocks)]
        x = jnp.concatenate(x, axis=1).astype(jnp.bfloat16)
        acc = acc + lax.dot_general(x, x, (((1,), (1,)), ((), ())), preferred_element_type=jnp.float32)
    out_ref[...] = jnp.concatenate([acc, jnp.zeros((total, EDGE - total), jnp.float32)], axis=1)


def solve_kernel(count, fit, local_ref, out_ref, send, held, send_sem, recv_sem):
    me = lax.axis_index("stripe")
    steps = []
    d = 1
    while d < count:
        steps.append(d)
        d *= 2
    partners = [me + d * (1 - 2 * ((me // d) % 2)) for d in steps]
    barrier = pltpu.get_barrier_semaphore()
    for partner in partners:
        pl.semaphore_signal(barrier, inc=1, device_id={"stripe": partner}, device_id_type=MESH)
    pl.semaphore_wait(barrier, len(partners))
    total = local_ref[...]
    for s, partner in enumerate(partners):
        source = local_ref
        if s:
            send[s] = total
            source = send.at[s]
        copy = pltpu.make_async_remote_copy(
            src_ref=source,
            dst_ref=held.at[s],
            send_sem=send_sem.at[s],
            recv_sem=recv_sem.at[s],
            device_id={"stripe": partner},
            device_id_type=MESH,
        )
        copy.start()
        copy.wait()
        total = total + held[s]
    a = total[:fit, :]
    sub = lax.broadcasted_iota(jnp.int32, a.shape, 0)
    for first in range(0, fit, BLOCK):
        block = range(first, min(first + BLOCK, fit))
        cols = [jnp.broadcast_to(a[:, k : k + 1], a.shape) for k in block]
        for t, k in enumerate(block):
            inverse = pl.reciprocal(cols[t][k : k + 1, :])
            row = a[k : k + 1, :] * inverse
            a = jnp.where(sub == k, row, a - cols[t] * row)
            for w in range(t + 1, len(block)):
                factor = cols[w][k : k + 1, :] * inverse
                cols[w] = jnp.where(sub == k, factor, cols[w] - cols[t] * factor)
    answer = jnp.broadcast_to(a[:, fit : fit + 1], a.shape)
    out_ref[...] = jnp.zeros_like(out_ref)
    out_ref[:fit, :] = answer


def model_kernel(region_rows, coef_ref, ext_ref, exp_ref, mask_ref, edge_ref, rowf_ref, colf_ref, out_ref, row_ref, band, wide_y, diff):
    rows, cols = out_ref.shape
    bases, taps = rowf_ref.shape
    fit = 3 * bases + 7
    tall = diff.shape[0]
    answer = coef_ref[:fit, :fit]
    same = lax.broadcasted_iota(jnp.int32, (fit, fit), 0) == lax.broadcasted_iota(jnp.int32, (fit, fit), 1)
    row_ref[...] = jnp.sum(jnp.where(same, answer, 0.0), axis=0, keepdims=True)
    ext_rows, wide = ext_ref.shape
    first = (lax.axis_index("stripe") * rows - 1).astype(jnp.float32)
    v = row_coords(first, tall, region_rows)
    rowf = jnp.concatenate([rowf_ref[...], jnp.zeros((bases, EDGE - taps), jnp.float32)], axis=1)
    colf = jnp.concatenate([colf_ref[...], jnp.zeros((bases, EDGE - taps), jnp.float32)], axis=1)
    start = ext_rows // 2 - rows // 2 - HALF - 1
    mats = []
    for t in range(3):
        c = coef_ref[pl.ds(t, bases, stride=3), :]
        mats.append(
            lax.dot_general(
                colf * c,
                rowf,
                (((0,), (0,)), ((), ())),
                precision=HIGHEST,
                preferred_element_type=jnp.float32,
            )
        )
    for j in range(taps):
        k0, k1, k2 = (jnp.broadcast_to(m[j : j + 1, :], (tall, EDGE)) for m in mats)
        main = k0 + v * k2 + (-(j - HALF) * 2.0 / cols) * k1
        main = shifted_rows(main, tall, start)
        side = shifted_rows(k1, tall, start + ext_rows)
        band[j * tall : (j + 1) * tall, :] = main + side
    ext = ext_ref[...]
    u_wide = col_coords(-float(EDGE), wide, cols)
    both = jnp.concatenate([ext, ext * u_wide, jnp.zeros((EDGE - 2 * ext_rows, wide), jnp.float32)], axis=0)
    high, rest = split(both)
    w_high, w_rest = split(band[...])
    dot = functools.partial(jnp.dot, preferred_element_type=jnp.float32)
    wide_y[...] = dot(w_high, high) + (dot(w_high, rest) + dot(w_rest, high))
    u = col_coords(0.0, cols, cols)
    q = [coef_ref[3 * bases + m : 3 * bases + m + 1, 0:1] for m in range(7)]
    terms = background(u, v)
    level = q[0] + q[1] * terms[1] + q[4] * terms[4]
    model = level + (q[2] * terms[2] + q[5] * terms[5]) + u * (q[3] * v + q[6] * terms[5])
    for j in range(taps):
        y = wide_y[j * tall : (j + 1) * tall, :]
        model = model + pltpu.roll(y, wide - (EDGE - HALF) - j, 1)[:, :cols]
    spare = jnp.zeros((tall - rows - 2, cols), jnp.float32)
    science = jnp.concatenate([edge_ref[0, 0:1, :], exp_ref[...], edge_ref[1, 0:1, :], spare], axis=0)
    good = jnp.concatenate(
        [edge_ref[0, 1:2, :], mask_ref[...].astype(jnp.float32), edge_ref[1, 1:2, :], spare], axis=0
    )
    diff[...] = good * (science - model)
    lane = lax.broadcasted_iota(jnp.int32, (rows, cols), 1)
    mid = diff[1 : rows + 1, :]
    left = jnp.where(lane == 0, 0.0, pltpu.roll(mid, 1, 1))
    right = jnp.where(lane == cols - 1, 0.0, pltpu.roll(mid, cols - 1, 1))
    around = diff[2 : rows + 2, :] + diff[0:rows, :] + right + left
    out_ref[...] = 4.0 * mid - around


def halo_kernel(count, tmpl_ref, exp_ref, mask_ref, ext_ref, edge_ref, parts, whole, extra_send, extra_recv, edge_send, edge_recv, send_sem, recv_sem):
    me = lax.axis_index("stripe")
    core = lax.axis_index("exp")
    rows, half = tmpl_ref.shape
    has_up = me > 0
    has_down = me < count - 1

    def copy(src, dst, n, stripe, exp):
        return pltpu.make_async_remote_copy(
            src_ref=src,
            dst_ref=dst,
            send_sem=send_sem.at[n],
            recv_sem=recv_sem.at[n],
            device_id={"stripe": stripe, "exp": exp},
            device_id_type=MESH,
        )

    def sends(way, stripe, tile):
        base = 5 * way
        return [
            copy(edge_send.at[way], edge_recv.at[way], base, stripe, core),
            copy(extra_send.at[way], extra_recv.at[2 * way], base + 1, stripe, core),
            copy(extra_send.at[way], extra_recv.at[2 * way + 1], base + 2, stripe, 1 - core),
            copy(tile, parts.at[2 * way], base + 3, stripe, core),
            copy(tile, parts.at[2 * way + 1], base + 4, stripe, 1 - core),
        ]

    def downs():
        return sends(0, me + 1, tmpl_ref.at[rows - TILE : rows])

    def ups():
        return sends(1, me - 1, tmpl_ref.at[0:TILE])

    more = HALF + 1 - TILE
    extra_send[0] = tmpl_ref[rows - TILE - more : rows - TILE, :]
    extra_send[1] = tmpl_ref[TILE : TILE + more, :]
    edge_send[0, 0:1, :] = exp_ref[rows - 1 : rows, :]
    edge_send[0, 1:2, :] = mask_ref[rows - 1 : rows, :].astype(jnp.float32)
    edge_send[1, 0:1, :] = exp_ref[0:1, :]
    edge_send[1, 1:2, :] = mask_ref[0:1, :].astype(jnp.float32)
    barrier = pltpu.get_barrier_semaphore()

    def greet(stripe, exp):
        pl.semaphore_signal(barrier, inc=1, device_id={"stripe": stripe, "exp": exp}, device_id_type=MESH)

    @pl.when(has_up)
    def _():
        greet(me - 1, core)
        greet(me - 1, 1 - core)

    @pl.when(has_down)
    def _():
        greet(me + 1, core)
        greet(me + 1, 1 - core)

    greet(me, 1 - core)
    pl.semaphore_wait(barrier, 1 + 2 * has_up.astype(jnp.int32) + 2 * has_down.astype(jnp.int32))

    @pl.when(has_down)
    def _():
        for c in downs():
            c.start()

    @pl.when(has_up)
    def _():
        for c in ups():
            c.start()

    across = copy(tmpl_ref, whole, 10, me, 1 - core)
    across.start()
    ext_ref[...] = jnp.zeros_like(ext_ref)
    edge_ref[...] = jnp.zeros_like(edge_ref)
    mine = pl.ds(pl.multiple_of(EDGE + core * half, EDGE), half)
    theirs = pl.ds(pl.multiple_of(EDGE + (1 - core) * half, EDGE), half)
    ext_ref[rows : 2 * rows, mine] = tmpl_ref[...]
    across.wait()
    ext_ref[rows : 2 * rows, theirs] = whole[...]

    @pl.when(has_up)
    def _():
        for c in downs():
            c.wait_recv()
        edge_ref[0] = edge_recv[0]
        for n, lanes in enumerate((mine, theirs)):
            ext_ref[rows - TILE : rows, lanes] = parts[n]
            ext_ref[rows - TILE - more : rows - TILE, lanes] = extra_recv[n]

    @pl.when(has_down)
    def _():
        for c in ups():
            c.wait_recv()
        edge_ref[1] = edge_recv[1]
        for n, lanes in enumerate((mine, theirs)):
            ext_ref[2 * rows : 2 * rows + TILE, lanes] = parts[2 + n]
            ext_ref[2 * rows + TILE : 2 * rows + TILE + more, lanes] = extra_recv[2 + n]

    @pl.when(has_down)
    def _():
        for c in downs():
            c.wait_send()

    @pl.when(has_up)
    def _():
        for c in ups():
            c.wait_send()


def shards(template, exposure, cosmic_mask, stamp_blocks, row_filters, col_filters):
    rows, cols = exposure.shape[1:]
    bases, taps = row_filters.shape
    fit = 3 * bases + 7
    stripes = lax.axis_size("stripe")
    region_rows = rows * stripes
    own_exp = exposure[0]
    own_mask = cosmic_mask[0]
    half = template.shape[1]
    ext_rows = 3 * rows
    wide = cols + 2 * EDGE
    tall = round_up(rows + 2, 8)
    total = round_up(fit + 1, 8)
    vmem = pl.BlockSpec(memory_space=pltpu.VMEM)
    smem = pl.BlockSpec(memory_space=pltpu.SMEM)
    f32 = jnp.float32
    ext, edges = pl.pallas_call(
        functools.partial(halo_kernel, stripes),
        out_shape=(jax.ShapeDtypeStruct((ext_rows, wide), f32), jax.ShapeDtypeStruct((2, 2, cols), f32)),
        in_specs=[vmem] * 3,
        out_specs=(vmem, vmem),
        scratch_shapes=[
            pltpu.VMEM((4, TILE, half), f32),
            pltpu.VMEM((rows, half), f32),
            pltpu.VMEM((2, HALF + 1 - TILE, half), f32),
            pltpu.VMEM((4, HALF + 1 - TILE, half), f32),
            pltpu.VMEM((2, 2, cols), f32),
            pltpu.VMEM((2, 2, cols), f32),
            pltpu.SemaphoreType.DMA((11,)),
            pltpu.SemaphoreType.DMA((11,)),
        ],
        compiler_params=pltpu.CompilerParams(collective_id=1, has_side_effects=True),
        name="halo",
    )(template, own_exp, own_mask)
    normal = pl.pallas_call(
        functools.partial(normal_kernel, float(region_rows)),
        out_shape=jax.ShapeDtypeStruct((total, EDGE), f32),
        in_specs=[vmem] * 3 + [smem] + [vmem] * 2,
        out_specs=vmem,
        scratch_shapes=[
            pltpu.VMEM((bases * rows, 2 * EDGE), f32),
            pltpu.VMEM((bases * rows, cols), f32),
            pltpu.VMEM((cols // (2 * EDGE), total * rows, EDGE), f32),
        ],
        name="normal",
    )(ext, own_exp, own_mask, stamp_blocks, row_filters, col_filters)
    hops = max(1, (stripes - 1).bit_length())
    coef = pl.pallas_call(
        functools.partial(solve_kernel, stripes, fit),
        out_shape=jax.ShapeDtypeStruct((total, EDGE), f32),
        in_specs=[vmem],
        out_specs=vmem,
        scratch_shapes=[
            pltpu.VMEM((hops, total, EDGE), f32),
            pltpu.VMEM((hops, total, EDGE), f32),
            pltpu.SemaphoreType.DMA((hops,)),
            pltpu.SemaphoreType.DMA((hops,)),
        ],
        compiler_params=pltpu.CompilerParams(collective_id=0, has_side_effects=True),
        name="solve",
    )(normal)
    filtered, coef_row = pl.pallas_call(
        functools.partial(model_kernel, float(region_rows)),
        out_shape=(jax.ShapeDtypeStruct((rows, cols), f32), jax.ShapeDtypeStruct((1, fit), f32)),
        in_specs=[vmem] * 7,
        out_specs=(vmem, vmem),
        scratch_shapes=[
            pltpu.VMEM((taps * tall, EDGE), f32),
            pltpu.VMEM((taps * tall, wide), f32),
            pltpu.VMEM((tall, cols), f32),
        ],
        name="model",
    )(coef, ext, own_exp, own_mask, edges, row_filters, col_filters)
    return (filtered[None], coef_row)


def solution(mesh):
    placed = (
        P(("groups", "stripe"), "exp"),
        P(("groups", "exp"), "stripe", None),
        P(("groups", "exp"), "stripe", None),
        P(("groups", "stripe"), None),
        P(),
        P(),
    )
    return jax.shard_map(
        shards,
        mesh=mesh,
        in_specs=placed,
        out_specs=(P(("groups", "exp"), "stripe", None), P(("groups", "exp"), None)),
        check_vma=False,
    )
```

```python
import functools

import jax
import jax.numpy as jnp
from jax import lax
from jax.experimental import pallas as pl
from jax.experimental.pallas import tpu as pltpu
from jax.sharding import PartitionSpec as P

HALF = 9
STAMP_W = 64
EDGE = 128
TILE = 8
BLOCK = 8
HIGHEST = lax.Precision.HIGHEST
MESH = pl.DeviceIdType.MESH


def round_up(n, m):
    return -(-n // m) * m


def row_coords(first, count, region_rows):
    index = lax.broadcasted_iota(jnp.int32, (count, 1), 0).astype(jnp.float32) + first
    return (2.0 * index + 1.0) / region_rows - 1.0


def col_coords(first, count, col_total):
    index = lax.broadcasted_iota(jnp.int32, (1, count), 1).astype(jnp.float32) + first
    return (2.0 * index + 1.0) / col_total - 1.0


def background(u, v):
    uu = 0.5 * (3.0 * u * u - 1.0)
    vv = 0.5 * (3.0 * v * v - 1.0)
    return [None, u, v, u * v, uu, vv, u * vv]


def split(x):
    high = x.astype(jnp.bfloat16)
    return high, (x - high.astype(jnp.float32)).astype(jnp.bfloat16)


def shifted_rows(row, count, start):
    return pltpu.roll(jnp.broadcast_to(row, (count, EDGE)), start, 1, stride=1, stride_axis=0)


def normal_kernel(region_rows, ext_ref, exp_ref, mask_ref, blk_ref, rowf_ref, colf_ref, out_ref, bandw, vert, design):
    bases, taps = rowf_ref.shape
    rows, cols = exp_ref.shape
    ext_rows = ext_ref.shape[0]
    fit = 3 * bases + 7
    total = out_ref.shape[0]
    half_cols = cols // 2
    blocks = half_cols // EDGE
    stamps = 2 * blocks
    low = lax.broadcasted_iota(jnp.int32, (1, EDGE), 1) < STAMP_W
    parity = [blk_ref[0, s] % 2 == 1 for s in range(stamps)]
    lanes = jnp.zeros((1, EDGE - taps), jnp.float32)

    windows = []
    for s in range(stamps):
        part = ext_ref[:, s * EDGE : (s + 3) * EDGE]
        early = pltpu.roll(part, 2 * EDGE + HALF, 1)[:, :EDGE]
        late = pltpu.roll(part, 2 * EDGE + HALF - STAMP_W, 1)[:, :EDGE]
        windows.append(jnp.where(parity[s], late, early))
    window = jnp.concatenate(windows, axis=1)
    w_high, w_rest = split(window)
    gap = jnp.zeros((EDGE - 2 * ext_rows, window.shape[1]), jnp.bfloat16)
    gap2 = jnp.zeros((EDGE - ext_rows, window.shape[1]), jnp.bfloat16)
    stacked = jnp.concatenate([w_high, w_rest, gap, w_high, gap2], axis=0)
    start = ext_rows // 2 - rows // 2 - HALF
    for b in range(bases):
        row = jnp.concatenate([rowf_ref[b : b + 1, :], lanes], axis=1)
        high = row.astype(jnp.bfloat16).astype(jnp.float32)
        twice = shifted_rows(high, rows, start) + shifted_rows(high, rows, start + ext_rows)
        rest = shifted_rows(row - high, rows, start)
        bandw[b * rows : (b + 1) * rows, :] = jnp.concatenate([twice, rest], axis=1)
    vert[...] = jnp.dot(bandw[...].astype(jnp.bfloat16), stacked, preferred_element_type=jnp.float32)

    def pick(x):
        parts = []
        for m in range(blocks):
            a = x[:, 2 * m * EDGE : (2 * m + 1) * EDGE]
            b = x[:, (2 * m + 1) * EDGE : (2 * m + 2) * EDGE]
            a = jnp.where(parity[2 * m], pltpu.roll(a, STAMP_W, 1), a)
            b = jnp.where(parity[2 * m + 1], b, pltpu.roll(b, STAMP_W, 1))
            parts.append(jnp.where(low, a, b))
        return jnp.concatenate(parts, axis=1)

    first = (lax.axis_index("stripe") * rows).astype(jnp.float32)
    v = jnp.broadcast_to(row_coords(first, rows, region_rows), (rows, half_cols))
    u_all = jnp.broadcast_to(col_coords(0.0, cols, cols), (8, cols))
    u = jnp.broadcast_to(pick(u_all)[0:1], (rows, half_cols))
    good = pick(mask_ref[...].astype(jnp.float32))

    def put(n, x):
        x = x * good
        for m in range(blocks):
            design[m, n * rows : (n + 1) * rows, :] = x[:, m * EDGE : (m + 1) * EDGE]

    for b in range(bases):
        x = vert[b * rows : (b + 1) * rows, :]
        x = jnp.concatenate([x[:, s * EDGE : (s + 1) * EDGE] for s in range(stamps)], axis=0)
        x_high, x_rest = split(x)
        row = jnp.concatenate([colf_ref[b : b + 1, :], lanes], axis=1)
        t_high, t_rest = split(shifted_rows(row, STAMP_W, 0))
        upper = jnp.concatenate([t_high, t_high], axis=1)
        lower = jnp.concatenate([t_rest, jnp.zeros_like(t_rest)], axis=1)
        y = lax.dot_general(
            jnp.concatenate([x_high, x_rest], axis=1),
            jnp.concatenate([upper, lower], axis=0),
            (((1,), (1,)), ((), ())),
            preferred_element_type=jnp.float32,
        )
        y = y + pltpu.roll(y, STAMP_W, 1)
        picked = jnp.concatenate(
            [
                jnp.where(low, y[2 * m * rows : (2 * m + 1) * rows], y[(2 * m + 1) * rows : (2 * m + 2) * rows])
                for m in range(blocks)
            ],
            axis=1,
        )
        put(3 * b, picked)
        put(3 * b + 1, picked * u)
        put(3 * b + 2, picked * v)

    terms = background(u, v)
    terms[0] = jnp.ones_like(u)
    for m, term in enumerate(terms):
        put(3 * bases + m, term)
    put(fit, pick(exp_ref[...]))
    for n in range(fit + 1, total):
        put(n, jnp.zeros_like(u))
    acc = jnp.zeros((total, total), jnp.float32)
    for r in range(rows):
        x = [design[m, pl.ds(r, total, stride=rows), :] for m in range(blocks)]
        x = jnp.concatenate(x, axis=1).astype(jnp.bfloat16)
        acc = acc + lax.dot_general(x, x, (((1,), (1,)), ((), ())), preferred_element_type=jnp.float32)
    out_ref[...] = jnp.concatenate([acc, jnp.zeros((total, EDGE - total), jnp.float32)], axis=1)


def fit_kernel(
    count,
    fit,
    region_rows,
    ext_ref,
    exp_ref,
    mask_ref,
    blk_ref,
    rowf_ref,
    colf_ref,
    out_ref,
    local_ref,
    bandw,
    vert,
    design,
    send,
    held,
    send_sem,
    recv_sem,
):
    me = lax.axis_index("stripe")
    steps = []
    d = 1
    while d < count:
        steps.append(d)
        d *= 2
    partners = [me + d * (1 - 2 * ((me // d) % 2)) for d in steps]
    barrier = pltpu.get_barrier_semaphore()
    for partner in partners:
        pl.semaphore_signal(barrier, inc=1, device_id={"stripe": partner}, device_id_type=MESH)
    normal_kernel(
        region_rows, ext_ref, exp_ref, mask_ref, blk_ref, rowf_ref, colf_ref, local_ref, bandw, vert, design
    )
    pl.semaphore_wait(barrier, len(partners))
    total = local_ref[...]
    for s, partner in enumerate(partners):
        source = local_ref
        if s:
            send[s] = total
            source = send.at[s]
        copy = pltpu.make_async_remote_copy(
            src_ref=source,
            dst_ref=held.at[s],
            send_sem=send_sem.at[s],
            recv_sem=recv_sem.at[s],
            device_id={"stripe": partner},
            device_id_type=MESH,
        )
        copy.start()
        copy.wait()
        total = total + held[s]
    a = total[:fit, :]
    sub = lax.broadcasted_iota(jnp.int32, a.shape, 0)
    for first in range(0, fit, BLOCK):
        block = range(first, min(first + BLOCK, fit))
        cols = [jnp.broadcast_to(a[:, k : k + 1], a.shape) for k in block]
        for t, k in enumerate(block):
            inverse = pl.reciprocal(cols[t][k : k + 1, :])
            row = a[k : k + 1, :] * inverse
            a = jnp.where(sub == k, row, a - cols[t] * row)
            for w in range(t + 1, len(block)):
                factor = cols[w][k : k + 1, :] * inverse
                cols[w] = jnp.where(sub == k, factor, cols[w] - cols[t] * factor)
    answer = jnp.broadcast_to(a[:, fit : fit + 1], a.shape)
    out_ref[...] = jnp.zeros_like(out_ref)
    out_ref[:fit, :] = answer


def model_kernel(region_rows, coef_ref, ext_ref, exp_ref, mask_ref, edge_ref, rowf_ref, colf_ref, out_ref, row_ref, band, wide_y, diff):
    rows, cols = out_ref.shape
    bases, taps = rowf_ref.shape
    fit = 3 * bases + 7
    tall = diff.shape[0]
    answer = coef_ref[:fit, :fit]
    same = lax.broadcasted_iota(jnp.int32, (fit, fit), 0) == lax.broadcasted_iota(jnp.int32, (fit, fit), 1)
    row_ref[...] = jnp.sum(jnp.where(same, answer, 0.0), axis=0, keepdims=True)
    ext_rows, wide = ext_ref.shape
    first = (lax.axis_index("stripe") * rows - 1).astype(jnp.float32)
    v = row_coords(first, tall, region_rows)
    rowf = jnp.concatenate([rowf_ref[...], jnp.zeros((bases, EDGE - taps), jnp.float32)], axis=1)
    colf = jnp.concatenate([colf_ref[...], jnp.zeros((bases, EDGE - taps), jnp.float32)], axis=1)
    start = ext_rows // 2 - rows // 2 - HALF - 1
    mats = []
    for t in range(3):
        c = coef_ref[pl.ds(t, bases, stride=3), :]
        mats.append(
            lax.dot_general(
                colf * c,
                rowf,
                (((0,), (0,)), ((), ())),
                precision=HIGHEST,
                preferred_element_type=jnp.float32,
            )
        )
    for j in range(taps):
        k0, k1, k2 = (jnp.broadcast_to(m[j : j + 1, :], (tall, EDGE)) for m in mats)
        main = k0 + v * k2 + (-(j - HALF) * 2.0 / cols) * k1
        main = shifted_rows(main, tall, start)
        side = shifted_rows(k1, tall, start + ext_rows)
        band[j * tall : (j + 1) * tall, :] = main + side
    ext = ext_ref[...]
    u_wide = col_coords(-float(EDGE), wide, cols)
    both = jnp.concatenate([ext, ext * u_wide, jnp.zeros((EDGE - 2 * ext_rows, wide), jnp.float32)], axis=0)
    high, rest = split(both)
    w_high, w_rest = split(band[...])
    dot = functools.partial(jnp.dot, preferred_element_type=jnp.float32)
    wide_y[...] = dot(w_high, high) + (dot(w_high, rest) + dot(w_rest, high))
    u = col_coords(0.0, cols, cols)
    q = [coef_ref[3 * bases + m : 3 * bases + m + 1, 0:1] for m in range(7)]
    terms = background(u, v)
    level = q[0] + q[1] * terms[1] + q[4] * terms[4]
    model = level + (q[2] * terms[2] + q[5] * terms[5]) + u * (q[3] * v + q[6] * terms[5])
    for j in range(taps):
        y = wide_y[j * tall : (j + 1) * tall, :]
        model = model + pltpu.roll(y, wide - (EDGE - HALF) - j, 1)[:, :cols]
    spare = jnp.zeros((tall - rows - 2, cols), jnp.float32)
    science = jnp.concatenate([edge_ref[0, 0:1, :], exp_ref[...], edge_ref[1, 0:1, :], spare], axis=0)
    good = jnp.concatenate(
        [edge_ref[0, 1:2, :], mask_ref[...].astype(jnp.float32), edge_ref[1, 1:2, :], spare], axis=0
    )
    diff[...] = good * (science - model)
    lane = lax.broadcasted_iota(jnp.int32, (rows, cols), 1)
    mid = diff[1 : rows + 1, :]
    left = jnp.where(lane == 0, 0.0, pltpu.roll(mid, 1, 1))
    right = jnp.where(lane == cols - 1, 0.0, pltpu.roll(mid, cols - 1, 1))
    around = diff[2 : rows + 2, :] + diff[0:rows, :] + right + left
    out_ref[...] = 4.0 * mid - around


def halo_kernel(count, tmpl_ref, exp_ref, mask_ref, ext_ref, edge_ref, parts, whole, extra_send, extra_recv, edge_send, edge_recv, send_sem, recv_sem):
    me = lax.axis_index("stripe")
    core = lax.axis_index("exp")
    rows, half = tmpl_ref.shape
    has_up = me > 0
    has_down = me < count - 1

    def copy(src, dst, n, stripe, exp):
        return pltpu.make_async_remote_copy(
            src_ref=src,
            dst_ref=dst,
            send_sem=send_sem.at[n],
            recv_sem=recv_sem.at[n],
            device_id={"stripe": stripe, "exp": exp},
            device_id_type=MESH,
        )

    def sends(way, stripe, tile):
        base = 5 * way
        return [
            copy(edge_send.at[way], edge_recv.at[way], base, stripe, core),
            copy(extra_send.at[way], extra_recv.at[2 * way], base + 1, stripe, core),
            copy(extra_send.at[way], extra_recv.at[2 * way + 1], base + 2, stripe, 1 - core),
            copy(tile, parts.at[2 * way], base + 3, stripe, core),
            copy(tile, parts.at[2 * way + 1], base + 4, stripe, 1 - core),
        ]

    def downs():
        return sends(0, me + 1, tmpl_ref.at[rows - TILE : rows])

    def ups():
        return sends(1, me - 1, tmpl_ref.at[0:TILE])

    more = HALF + 1 - TILE
    extra_send[0] = tmpl_ref[rows - TILE - more : rows - TILE, :]
    extra_send[1] = tmpl_ref[TILE : TILE + more, :]
    edge_send[0, 0:1, :] = exp_ref[rows - 1 : rows, :]
    edge_send[0, 1:2, :] = mask_ref[rows - 1 : rows, :].astype(jnp.float32)
    edge_send[1, 0:1, :] = exp_ref[0:1, :]
    edge_send[1, 1:2, :] = mask_ref[0:1, :].astype(jnp.float32)
    barrier = pltpu.get_barrier_semaphore()

    def greet(stripe, exp):
        pl.semaphore_signal(barrier, inc=1, device_id={"stripe": stripe, "exp": exp}, device_id_type=MESH)

    @pl.when(has_up)
    def _():
        greet(me - 1, core)
        greet(me - 1, 1 - core)

    @pl.when(has_down)
    def _():
        greet(me + 1, core)
        greet(me + 1, 1 - core)

    greet(me, 1 - core)
    pl.semaphore_wait(barrier, 1 + 2 * has_up.astype(jnp.int32) + 2 * has_down.astype(jnp.int32))

    @pl.when(has_down)
    def _():
        for c in downs():
            c.start()

    @pl.when(has_up)
    def _():
        for c in ups():
            c.start()

    across = copy(tmpl_ref, whole, 10, me, 1 - core)
    across.start()
    ext_ref[...] = jnp.zeros_like(ext_ref)
    edge_ref[...] = jnp.zeros_like(edge_ref)
    mine = pl.ds(pl.multiple_of(EDGE + core * half, EDGE), half)
    theirs = pl.ds(pl.multiple_of(EDGE + (1 - core) * half, EDGE), half)
    ext_ref[rows : 2 * rows, mine] = tmpl_ref[...]
    across.wait()
    ext_ref[rows : 2 * rows, theirs] = whole[...]

    @pl.when(has_up)
    def _():
        for c in downs():
            c.wait_recv()
        edge_ref[0] = edge_recv[0]
        for n, lanes in enumerate((mine, theirs)):
            ext_ref[rows - TILE : rows, lanes] = parts[n]
            ext_ref[rows - TILE - more : rows - TILE, lanes] = extra_recv[n]

    @pl.when(has_down)
    def _():
        for c in ups():
            c.wait_recv()
        edge_ref[1] = edge_recv[1]
        for n, lanes in enumerate((mine, theirs)):
            ext_ref[2 * rows : 2 * rows + TILE, lanes] = parts[2 + n]
            ext_ref[2 * rows + TILE : 2 * rows + TILE + more, lanes] = extra_recv[2 + n]

    @pl.when(has_down)
    def _():
        for c in downs():
            c.wait_send()

    @pl.when(has_up)
    def _():
        for c in ups():
            c.wait_send()


def shards(template, exposure, cosmic_mask, stamp_blocks, row_filters, col_filters):
    rows, cols = exposure.shape[1:]
    bases, taps = row_filters.shape
    fit = 3 * bases + 7
    stripes = lax.axis_size("stripe")
    region_rows = rows * stripes
    own_exp = exposure[0]
    own_mask = cosmic_mask[0]
    half = template.shape[1]
    ext_rows = 3 * rows
    wide = cols + 2 * EDGE
    tall = round_up(rows + 2, 8)
    total = round_up(fit + 1, 8)
    vmem = pl.BlockSpec(memory_space=pltpu.VMEM)
    smem = pl.BlockSpec(memory_space=pltpu.SMEM)
    f32 = jnp.float32
    ext, edges = pl.pallas_call(
        functools.partial(halo_kernel, stripes),
        out_shape=(jax.ShapeDtypeStruct((ext_rows, wide), f32), jax.ShapeDtypeStruct((2, 2, cols), f32)),
        in_specs=[vmem] * 3,
        out_specs=(vmem, vmem),
        scratch_shapes=[
            pltpu.VMEM((4, TILE, half), f32),
            pltpu.VMEM((rows, half), f32),
            pltpu.VMEM((2, HALF + 1 - TILE, half), f32),
            pltpu.VMEM((4, HALF + 1 - TILE, half), f32),
            pltpu.VMEM((2, 2, cols), f32),
            pltpu.VMEM((2, 2, cols), f32),
            pltpu.SemaphoreType.DMA((11,)),
            pltpu.SemaphoreType.DMA((11,)),
        ],
        compiler_params=pltpu.CompilerParams(collective_id=1, has_side_effects=True),
        name="halo",
    )(template, own_exp, own_mask)
    hops = max(1, (stripes - 1).bit_length())
    coef = pl.pallas_call(
        functools.partial(fit_kernel, stripes, fit, float(region_rows)),
        out_shape=jax.ShapeDtypeStruct((total, EDGE), f32),
        in_specs=[vmem] * 3 + [smem] + [vmem] * 2,
        out_specs=vmem,
        scratch_shapes=[
            pltpu.VMEM((total, EDGE), f32),
            pltpu.VMEM((bases * rows, 2 * EDGE), f32),
            pltpu.VMEM((bases * rows, cols), f32),
            pltpu.VMEM((cols // (2 * EDGE), total * rows, EDGE), f32),
            pltpu.VMEM((hops, total, EDGE), f32),
            pltpu.VMEM((hops, total, EDGE), f32),
            pltpu.SemaphoreType.DMA((hops,)),
            pltpu.SemaphoreType.DMA((hops,)),
        ],
        compiler_params=pltpu.CompilerParams(collective_id=0, has_side_effects=True),
        name="fit",
    )(ext, own_exp, own_mask, stamp_blocks, row_filters, col_filters)
    filtered, coef_row = pl.pallas_call(
        functools.partial(model_kernel, float(region_rows)),
        out_shape=(jax.ShapeDtypeStruct((rows, cols), f32), jax.ShapeDtypeStruct((1, fit), f32)),
        in_specs=[vmem] * 7,
        out_specs=(vmem, vmem),
        scratch_shapes=[
            pltpu.VMEM((taps * tall, EDGE), f32),
            pltpu.VMEM((taps * tall, wide), f32),
            pltpu.VMEM((tall, cols), f32),
        ],
        name="model",
    )(coef, ext, own_exp, own_mask, edges, row_filters, col_filters)
    return (filtered[None], coef_row)


def solution(mesh):
    placed = (
        P(("groups", "stripe"), "exp"),
        P(("groups", "exp"), "stripe", None),
        P(("groups", "exp"), "stripe", None),
        P(("groups", "stripe"), None),
        P(),
        P(),
    )
    return jax.shard_map(
        shards,
        mesh=mesh,
        in_specs=placed,
        out_specs=(P(("groups", "exp"), "stripe", None), P(("groups", "exp"), None)),
        check_vma=False,
    )
```

```python
import functools

import jax
import jax.numpy as jnp
from jax import lax
from jax.experimental import pallas as pl
from jax.experimental.pallas import tpu as pltpu
from jax.sharding import PartitionSpec as P

HALF = 9
STAMP_W = 64
EDGE = 128
TILE = 8
BLOCK = 8
HIGHEST = lax.Precision.HIGHEST
MESH = pl.DeviceIdType.MESH


def round_up(n, m):
    return -(-n // m) * m


def row_coords(first, count, region_rows):
    index = lax.broadcasted_iota(jnp.int32, (count, 1), 0).astype(jnp.float32) + first
    return (2.0 * index + 1.0) / region_rows - 1.0


def col_coords(first, count, col_total):
    index = lax.broadcasted_iota(jnp.int32, (1, count), 1).astype(jnp.float32) + first
    return (2.0 * index + 1.0) / col_total - 1.0


def background(u, v):
    uu = 0.5 * (3.0 * u * u - 1.0)
    vv = 0.5 * (3.0 * v * v - 1.0)
    return [None, u, v, u * v, uu, vv, u * vv]


def split(x):
    high = x.astype(jnp.bfloat16)
    return high, (x - high.astype(jnp.float32)).astype(jnp.bfloat16)


def shifted_rows(row, count, start):
    return pltpu.roll(jnp.broadcast_to(row, (count, EDGE)), start, 1, stride=1, stride_axis=0)


def normal_kernel(region_rows, ext_ref, exp_ref, mask_ref, blk_ref, rowf_ref, colf_ref, out_ref, bandw, vert, design):
    bases, taps = rowf_ref.shape
    rows, cols = exp_ref.shape
    ext_rows = ext_ref.shape[0]
    fit = 3 * bases + 7
    total = out_ref.shape[0]
    half_cols = cols // 2
    blocks = half_cols // EDGE
    stamps = 2 * blocks
    low = lax.broadcasted_iota(jnp.int32, (1, EDGE), 1) < STAMP_W
    parity = [blk_ref[0, s] % 2 == 1 for s in range(stamps)]
    lanes = jnp.zeros((1, EDGE - taps), jnp.float32)

    windows = []
    for s in range(stamps):
        part = ext_ref[:, s * EDGE : (s + 3) * EDGE]
        early = pltpu.roll(part, 2 * EDGE + HALF, 1)[:, :EDGE]
        late = pltpu.roll(part, 2 * EDGE + HALF - STAMP_W, 1)[:, :EDGE]
        windows.append(jnp.where(parity[s], late, early))
    window = jnp.concatenate(windows, axis=1)
    w_high, w_rest = split(window)
    gap = jnp.zeros((EDGE - 2 * ext_rows, window.shape[1]), jnp.bfloat16)
    gap2 = jnp.zeros((EDGE - ext_rows, window.shape[1]), jnp.bfloat16)
    stacked = jnp.concatenate([w_high, w_rest, gap, w_high, gap2], axis=0)
    start = ext_rows // 2 - rows // 2 - HALF
    for b in range(bases):
        row = jnp.concatenate([rowf_ref[b : b + 1, :], lanes], axis=1)
        high = row.astype(jnp.bfloat16).astype(jnp.float32)
        twice = shifted_rows(high, rows, start) + shifted_rows(high, rows, start + ext_rows)
        rest = shifted_rows(row - high, rows, start)
        bandw[b * rows : (b + 1) * rows, :] = jnp.concatenate([twice, rest], axis=1)
    vert[...] = jnp.dot(bandw[...].astype(jnp.bfloat16), stacked, preferred_element_type=jnp.float32)

    def pick(x):
        parts = []
        for m in range(blocks):
            a = x[:, 2 * m * EDGE : (2 * m + 1) * EDGE]
            b = x[:, (2 * m + 1) * EDGE : (2 * m + 2) * EDGE]
            a = jnp.where(parity[2 * m], pltpu.roll(a, STAMP_W, 1), a)
            b = jnp.where(parity[2 * m + 1], b, pltpu.roll(b, STAMP_W, 1))
            parts.append(jnp.where(low, a, b))
        return jnp.concatenate(parts, axis=1)

    first = (lax.axis_index("stripe") * rows).astype(jnp.float32)
    v = jnp.broadcast_to(row_coords(first, rows, region_rows), (rows, half_cols))
    u_all = jnp.broadcast_to(col_coords(0.0, cols, cols), (8, cols))
    u = jnp.broadcast_to(pick(u_all)[0:1], (rows, half_cols))
    good = pick(mask_ref[...].astype(jnp.float32))

    def put(n, x):
        x = x * good
        for m in range(blocks):
            design[m, n * rows : (n + 1) * rows, :] = x[:, m * EDGE : (m + 1) * EDGE]

    for b in range(bases):
        x = vert[b * rows : (b + 1) * rows, :]
        x = jnp.concatenate([x[:, s * EDGE : (s + 1) * EDGE] for s in range(stamps)], axis=0)
        x_high, x_rest = split(x)
        row = jnp.concatenate([colf_ref[b : b + 1, :], lanes], axis=1)
        t_high, t_rest = split(shifted_rows(row, STAMP_W, 0))
        upper = jnp.concatenate([t_high, t_high], axis=1)
        lower = jnp.concatenate([t_rest, jnp.zeros_like(t_rest)], axis=1)
        y = lax.dot_general(
            jnp.concatenate([x_high, x_rest], axis=1),
            jnp.concatenate([upper, lower], axis=0),
            (((1,), (1,)), ((), ())),
            preferred_element_type=jnp.float32,
        )
        y = y + pltpu.roll(y, STAMP_W, 1)
        picked = jnp.concatenate(
            [
                jnp.where(low, y[2 * m * rows : (2 * m + 1) * rows], y[(2 * m + 1) * rows : (2 * m + 2) * rows])
                for m in range(blocks)
            ],
            axis=1,
        )
        put(3 * b, picked)
        put(3 * b + 1, picked * u)
        put(3 * b + 2, picked * v)

    terms = background(u, v)
    terms[0] = jnp.ones_like(u)
    for m, term in enumerate(terms):
        put(3 * bases + m, term)
    put(fit, pick(exp_ref[...]))
    for n in range(fit + 1, total):
        put(n, jnp.zeros_like(u))
    acc = jnp.zeros((total, total), jnp.float32)
    for r in range(rows):
        x = [design[m, pl.ds(r, total, stride=rows), :] for m in range(blocks)]
        x = jnp.concatenate(x, axis=1).astype(jnp.bfloat16)
        acc = acc + lax.dot_general(x, x, (((1,), (1,)), ((), ())), preferred_element_type=jnp.float32)
    out_ref[...] = jnp.concatenate([acc, jnp.zeros((total, EDGE - total), jnp.float32)], axis=1)


def exchange_halo(count, partners, tmpl_ref, exp_ref, mask_ref, ext_ref, edge_ref, parts, whole, extra_send, extra_recv, edge_send, edge_recv, send_sem, recv_sem):
    me = lax.axis_index("stripe")
    core = lax.axis_index("exp")
    rows, half = tmpl_ref.shape
    has_up = me > 0
    has_down = me < count - 1

    def copy(src, dst, n, stripe, exp):
        return pltpu.make_async_remote_copy(
            src_ref=src,
            dst_ref=dst,
            send_sem=send_sem.at[n],
            recv_sem=recv_sem.at[n],
            device_id={"stripe": stripe, "exp": exp},
            device_id_type=MESH,
        )

    def sends(way, stripe, tile):
        base = 5 * way
        return [
            copy(edge_send.at[way], edge_recv.at[way], base, stripe, core),
            copy(extra_send.at[way], extra_recv.at[2 * way], base + 1, stripe, core),
            copy(extra_send.at[way], extra_recv.at[2 * way + 1], base + 2, stripe, 1 - core),
            copy(tile, parts.at[2 * way], base + 3, stripe, core),
            copy(tile, parts.at[2 * way + 1], base + 4, stripe, 1 - core),
        ]

    def downs():
        return sends(0, me + 1, tmpl_ref.at[rows - TILE : rows])

    def ups():
        return sends(1, me - 1, tmpl_ref.at[0:TILE])

    more = HALF + 1 - TILE
    extra_send[0] = tmpl_ref[rows - TILE - more : rows - TILE, :]
    extra_send[1] = tmpl_ref[TILE : TILE + more, :]
    edge_send[0, 0:1, :] = exp_ref[rows - 1 : rows, :]
    edge_send[0, 1:2, :] = mask_ref[rows - 1 : rows, :].astype(jnp.float32)
    edge_send[1, 0:1, :] = exp_ref[0:1, :]
    edge_send[1, 1:2, :] = mask_ref[0:1, :].astype(jnp.float32)
    barrier = pltpu.get_barrier_semaphore()

    def greet(stripe, exp):
        pl.semaphore_signal(barrier, inc=1, device_id={"stripe": stripe, "exp": exp}, device_id_type=MESH)

    @pl.when(has_up)
    def _():
        greet(me - 1, core)
        greet(me - 1, 1 - core)

    @pl.when(has_down)
    def _():
        greet(me + 1, core)
        greet(me + 1, 1 - core)

    greet(me, 1 - core)
    for partner in partners:
        greet(partner, core)
    pl.semaphore_wait(barrier, 1 + len(partners) + 2 * has_up.astype(jnp.int32) + 2 * has_down.astype(jnp.int32))

    @pl.when(has_down)
    def _():
        for c in downs()[::-1]:
            c.start()

    @pl.when(has_up)
    def _():
        for c in ups()[::-1]:
            c.start()

    across = copy(tmpl_ref, whole, 10, me, 1 - core)
    across.start()
    ext_ref[...] = jnp.zeros_like(ext_ref)
    edge_ref[...] = jnp.zeros_like(edge_ref)
    mine = pl.ds(pl.multiple_of(EDGE + core * half, EDGE), half)
    theirs = pl.ds(pl.multiple_of(EDGE + (1 - core) * half, EDGE), half)
    ext_ref[rows : 2 * rows, mine] = tmpl_ref[...]
    across.wait()
    ext_ref[rows : 2 * rows, theirs] = whole[...]

    @pl.when(has_up)
    def _():
        for c in downs()[1:]:
            c.wait_recv()
        for n, lanes in enumerate((mine, theirs)):
            ext_ref[rows - TILE : rows, lanes] = parts[n]
            ext_ref[rows - TILE - more : rows - TILE, lanes] = extra_recv[n]

    @pl.when(has_down)
    def _():
        for c in ups()[1:]:
            c.wait_recv()
        for n, lanes in enumerate((mine, theirs)):
            ext_ref[2 * rows : 2 * rows + TILE, lanes] = parts[2 + n]
            ext_ref[2 * rows + TILE : 2 * rows + TILE + more, lanes] = extra_recv[2 + n]

    def finish():
        @pl.when(has_up)
        def _():
            downs()[0].wait_recv()
            edge_ref[0] = edge_recv[0]
            for c in ups():
                c.wait_send()

        @pl.when(has_down)
        def _():
            ups()[0].wait_recv()
            edge_ref[1] = edge_recv[1]
            for c in downs():
                c.wait_send()

    return finish


def fit_kernel(
    count,
    fit,
    region_rows,
    tmpl_ref,
    exp_ref,
    mask_ref,
    blk_ref,
    rowf_ref,
    colf_ref,
    out_ref,
    ext_ref,
    edge_ref,
    parts,
    whole,
    extra_send,
    extra_recv,
    edge_send,
    edge_recv,
    halo_send,
    halo_recv,
    local_ref,
    bandw,
    vert,
    design,
    send,
    held,
    send_sem,
    recv_sem,
):
    me = lax.axis_index("stripe")
    steps = []
    d = 1
    while d < count:
        steps.append(d)
        d *= 2
    partners = [me + d * (1 - 2 * ((me // d) % 2)) for d in steps]
    finish = exchange_halo(
        count,
        partners,
        tmpl_ref,
        exp_ref,
        mask_ref,
        ext_ref,
        edge_ref,
        parts,
        whole,
        extra_send,
        extra_recv,
        edge_send,
        edge_recv,
        halo_send,
        halo_recv,
    )
    normal_kernel(
        region_rows, ext_ref, exp_ref, mask_ref, blk_ref, rowf_ref, colf_ref, local_ref, bandw, vert, design
    )
    total = local_ref[...]
    for s, partner in enumerate(partners):
        source = local_ref
        if s:
            send[s] = total
            source = send.at[s]
        copy = pltpu.make_async_remote_copy(
            src_ref=source,
            dst_ref=held.at[s],
            send_sem=send_sem.at[s],
            recv_sem=recv_sem.at[s],
            device_id={"stripe": partner},
            device_id_type=MESH,
        )
        copy.start()
        copy.wait()
        total = total + held[s]
    a = total[:fit, :]
    sub = lax.broadcasted_iota(jnp.int32, a.shape, 0)
    for first in range(0, fit, BLOCK):
        block = range(first, min(first + BLOCK, fit))
        cols = [jnp.broadcast_to(a[:, k : k + 1], a.shape) for k in block]
        for t, k in enumerate(block):
            inverse = pl.reciprocal(cols[t][k : k + 1, :])
            row = a[k : k + 1, :] * inverse
            a = jnp.where(sub == k, row, a - cols[t] * row)
            for w in range(t + 1, len(block)):
                factor = cols[w][k : k + 1, :] * inverse
                cols[w] = jnp.where(sub == k, factor, cols[w] - cols[t] * factor)
    answer = jnp.broadcast_to(a[:, fit : fit + 1], a.shape)
    out_ref[...] = jnp.zeros_like(out_ref)
    out_ref[:fit, :] = answer
    finish()


def model_kernel(region_rows, coef_ref, ext_ref, exp_ref, mask_ref, edge_ref, rowf_ref, colf_ref, out_ref, row_ref, band, wide_y, diff):
    rows, cols = out_ref.shape
    bases, taps = rowf_ref.shape
    fit = 3 * bases + 7
    tall = diff.shape[0]
    answer = coef_ref[:fit, :fit]
    same = lax.broadcasted_iota(jnp.int32, (fit, fit), 0) == lax.broadcasted_iota(jnp.int32, (fit, fit), 1)
    row_ref[...] = jnp.sum(jnp.where(same, answer, 0.0), axis=0, keepdims=True)
    ext_rows, wide = ext_ref.shape
    first = (lax.axis_index("stripe") * rows - 1).astype(jnp.float32)
    v = row_coords(first, tall, region_rows)
    rowf = jnp.concatenate([rowf_ref[...], jnp.zeros((bases, EDGE - taps), jnp.float32)], axis=1)
    colf = jnp.concatenate([colf_ref[...], jnp.zeros((bases, EDGE - taps), jnp.float32)], axis=1)
    start = ext_rows // 2 - rows // 2 - HALF - 1
    mats = []
    for t in range(3):
        c = coef_ref[pl.ds(t, bases, stride=3), :]
        mats.append(
            lax.dot_general(
                colf * c,
                rowf,
                (((0,), (0,)), ((), ())),
                precision=HIGHEST,
                preferred_element_type=jnp.float32,
            )
        )
    for j in range(taps):
        k0, k1, k2 = (jnp.broadcast_to(m[j : j + 1, :], (tall, EDGE)) for m in mats)
        main = k0 + v * k2 + (-(j - HALF) * 2.0 / cols) * k1
        main = shifted_rows(main, tall, start)
        side = shifted_rows(k1, tall, start + ext_rows)
        band[j * tall : (j + 1) * tall, :] = main + side
    ext = ext_ref[...]
    u_wide = col_coords(-float(EDGE), wide, cols)
    both = jnp.concatenate([ext, ext * u_wide, jnp.zeros((EDGE - 2 * ext_rows, wide), jnp.float32)], axis=0)
    high, rest = split(both)
    w_high, w_rest = split(band[...])
    dot = functools.partial(jnp.dot, preferred_element_type=jnp.float32)
    wide_y[...] = dot(w_high, high) + (dot(w_high, rest) + dot(w_rest, high))
    u = col_coords(0.0, cols, cols)
    q = [coef_ref[3 * bases + m : 3 * bases + m + 1, 0:1] for m in range(7)]
    terms = background(u, v)
    level = q[0] + q[1] * terms[1] + q[4] * terms[4]
    model = level + (q[2] * terms[2] + q[5] * terms[5]) + u * (q[3] * v + q[6] * terms[5])
    for j in range(taps):
        y = wide_y[j * tall : (j + 1) * tall, :]
        model = model + pltpu.roll(y, wide - (EDGE - HALF) - j, 1)[:, :cols]
    spare = jnp.zeros((tall - rows - 2, cols), jnp.float32)
    science = jnp.concatenate([edge_ref[0, 0:1, :], exp_ref[...], edge_ref[1, 0:1, :], spare], axis=0)
    good = jnp.concatenate(
        [edge_ref[0, 1:2, :], mask_ref[...].astype(jnp.float32), edge_ref[1, 1:2, :], spare], axis=0
    )
    diff[...] = good * (science - model)
    lane = lax.broadcasted_iota(jnp.int32, (rows, cols), 1)
    mid = diff[1 : rows + 1, :]
    left = jnp.where(lane == 0, 0.0, pltpu.roll(mid, 1, 1))
    right = jnp.where(lane == cols - 1, 0.0, pltpu.roll(mid, cols - 1, 1))
    around = diff[2 : rows + 2, :] + diff[0:rows, :] + right + left
    out_ref[...] = 4.0 * mid - around


def shards(template, exposure, cosmic_mask, stamp_blocks, row_filters, col_filters):
    rows, cols = exposure.shape[1:]
    bases, taps = row_filters.shape
    fit = 3 * bases + 7
    stripes = lax.axis_size("stripe")
    region_rows = rows * stripes
    own_exp = exposure[0]
    own_mask = cosmic_mask[0]
    half = template.shape[1]
    ext_rows = 3 * rows
    wide = cols + 2 * EDGE
    tall = round_up(rows + 2, 8)
    total = round_up(fit + 1, 8)
    vmem = pl.BlockSpec(memory_space=pltpu.VMEM)
    smem = pl.BlockSpec(memory_space=pltpu.SMEM)
    f32 = jnp.float32
    hops = max(1, (stripes - 1).bit_length())
    coef, ext, edges = pl.pallas_call(
        functools.partial(fit_kernel, stripes, fit, float(region_rows)),
        out_shape=(
            jax.ShapeDtypeStruct((total, EDGE), f32),
            jax.ShapeDtypeStruct((ext_rows, wide), f32),
            jax.ShapeDtypeStruct((2, 2, cols), f32),
        ),
        in_specs=[vmem] * 3 + [smem] + [vmem] * 2,
        out_specs=(vmem, vmem, vmem),
        scratch_shapes=[
            pltpu.VMEM((4, TILE, half), f32),
            pltpu.VMEM((rows, half), f32),
            pltpu.VMEM((2, HALF + 1 - TILE, half), f32),
            pltpu.VMEM((4, HALF + 1 - TILE, half), f32),
            pltpu.VMEM((2, 2, cols), f32),
            pltpu.VMEM((2, 2, cols), f32),
            pltpu.SemaphoreType.DMA((11,)),
            pltpu.SemaphoreType.DMA((11,)),
            pltpu.VMEM((total, EDGE), f32),
            pltpu.VMEM((bases * rows, 2 * EDGE), f32),
            pltpu.VMEM((bases * rows, cols), f32),
            pltpu.VMEM((cols // (2 * EDGE), total * rows, EDGE), f32),
            pltpu.VMEM((hops, total, EDGE), f32),
            pltpu.VMEM((hops, total, EDGE), f32),
            pltpu.SemaphoreType.DMA((hops,)),
            pltpu.SemaphoreType.DMA((hops,)),
        ],
        compiler_params=pltpu.CompilerParams(collective_id=0, has_side_effects=True),
        name="fit",
    )(template, own_exp, own_mask, stamp_blocks, row_filters, col_filters)
    filtered, coef_row = pl.pallas_call(
        functools.partial(model_kernel, float(region_rows)),
        out_shape=(jax.ShapeDtypeStruct((rows, cols), f32), jax.ShapeDtypeStruct((1, fit), f32)),
        in_specs=[vmem] * 7,
        out_specs=(vmem, vmem),
        scratch_shapes=[
            pltpu.VMEM((taps * tall, EDGE), f32),
            pltpu.VMEM((taps * tall, wide), f32),
            pltpu.VMEM((tall, cols), f32),
        ],
        name="model",
    )(coef, ext, own_exp, own_mask, edges, row_filters, col_filters)
    return (filtered[None], coef_row)


def solution(mesh):
    placed = (
        P(("groups", "stripe"), "exp"),
        P(("groups", "exp"), "stripe", None),
        P(("groups", "exp"), "stripe", None),
        P(("groups", "stripe"), None),
        P(),
        P(),
    )
    return jax.shard_map(
        shards,
        mesh=mesh,
        in_specs=placed,
        out_specs=(P(("groups", "exp"), "stripe", None), P(("groups", "exp"), None)),
        check_vma=False,
    )
```
